32 devices in a mesh: groups: 2 (over x), enc: 16 (over z, y, core).
Axes of the slice: x: 2, y: 2, z: 4, core: 2. Of those that a mesh axis runs over, the one named last changes fastest.
Arguments:
- tiles: bfloat16 [16384, 4, 512], P(('groups', 'enc')), parts along dimension 0, may hold values from -8 to 8, as said below
- tile_counts: int32 [32, 4], P(('groups', 'enc')), parts along dimension 0, may hold values from 1 to 252, as said below
- assign: int32 [32, 512], P(('groups', 'enc')), parts along dimension 0, may hold values from 0 to 512, as said below
- labels: int32 [32, 4], P(('groups', 'enc')), parts along dimension 0, may hold values from 0 to 1
- w_conv: bfloat16 [512, 1024], replicated, may hold values from -0.25 to 0.25
- bn_gain: float32 [1024], replicated, may hold values from 0.5 to 1.5
- bn_shift: float32 [1024], replicated, may hold values from -3 to 3
- w_fc: bfloat16 [1024, 512], replicated, may hold values from -0.1875 to 0.1875
- w_gate: bfloat16 [512, 512], replicated, may hold values from -0.25 to 0.25
- w_score: float32 [256], replicated, may hold values from -0.3 to 0.3
- w_cls: float32 [512, 2], replicated, may hold values from -0.25 to 0.25
Outputs:
- loss: float32 [2], P('groups'), parts along dimension 0
- grad_conv: float32 [1024, 1024], P('groups'), parts along dimension 0
- grad_gain: float32 [2048], P('groups'), parts along dimension 0
- grad_shift: float32 [2048], P('groups'), parts along dimension 0
- grad_fc: float32 [2048, 512], P('groups'), parts along dimension 0
- grad_gate: float32 [1024, 512], P('groups'), parts along dimension 0
- grad_score: float32 [512], P('groups'), parts along dimension 0
- grad_cls: float32 [1024, 2], P('groups'), parts along dimension 0
The draws below stay inside these ranges and needn't reach their ends.
There are 2 independent parts, one for each index of `groups`. The reference program is written for one: setup_inputs(seed, part) draws one part's arguments, and reference() takes and returns one part's arrays. A program takes and returns all parts, laid end to end along the dimension named above; an argument that names none is the same for every part. Nothing has to cross between parts.
Inputs may be any that keep to these rules, and one draw needn't show every extreme that they name: `tile_counts`: each owner's counts sum to its number of tiles (the entries of its assign row below 512); each owner has one slide of exactly (tiles + 1) // 2 tiles; the busiest owner has 504 tiles. An owner's tiles take its first rows, and the rest of its row of assign is 512. Tile entries are distinct; slot // 32 is the encoder group. For every group e, row o names exactly the slots e * 32 to e * 32 + c - 1 for some c of 1 to 32; every group receives 264 tiles in all; some owner sends 32 tiles to some group. Owners hold uneven numbers of tiles, from 24 to 504. Real-valued tile features; rows past an owner's tiles are zero.
All inputs are finite; a program needn't handle non-finite values.
Results may differ from the reference program's by a relative error of at most 0.0055.
The reference program's roundings to bfloat16 on the way count: a program that leaves them out, or rounds other values in their place, can miss the bound.
Values may be sent and summed in bfloat16 or wider, within the bound.
No kernel may reach another device: no remote copies, remote signals or barrier semaphores. Data moves between devices by JAX's collectives and lax.ppermute only.
A program may use at most 64 MiB of HBM per device.

```python
import jax
import jax.numpy as jnp
from jax import lax

C_MID = 512
EMB = 1024
HID = 512
ATT = 256
CLASSES = 2
PIX = 4
SLOTS_DEV = 512
SL_DEV = 4
ENCODERS = 16
CAP = 32
TILES_DEV = 264


def owner_plan(key):
    level_key, extra_key = jax.random.split(jax.random.fold_in(key, 5))
    shuffled = jax.random.permutation(level_key, ENCODERS).astype(jnp.int32)
    level = 1 + shuffled % 4 * (CAP - 2) // 3
    extra = (jax.random.permutation(extra_key, ENCODERS) % 2).astype(jnp.int32)
    owner_total = ENCODERS * level + ENCODERS // 2
    return (level, extra, owner_total)


def draw_tiles(key, part):
    base_key, scale_key, offset_key = jax.random.split(jax.random.fold_in(key, 3), 3)
    tile_shape = (ENCODERS, SLOTS_DEV, PIX, C_MID)
    base = jnp.clip(jax.random.normal(base_key, tile_shape, jnp.float32), -4.0, 4.0)
    stain_scale = jnp.exp(jax.random.uniform(scale_key, (ENCODERS, 1, 1, 1), jnp.float32, -0.7, 0.7))
    offset = 0.6 * jnp.clip(jax.random.normal(offset_key, (ENCODERS, 1, 1, C_MID), jnp.float32), -3.0, 3.0)
    values = jnp.clip(base * stain_scale + offset, -8.0, 8.0)
    level, extra, owner_total = owner_plan(key)
    row_index = jnp.arange(SLOTS_DEV, dtype=jnp.int32)[None, :]
    live = (row_index < owner_total[:, None]).astype(jnp.float32)[:, :, None, None]
    values = values * live
    return values.reshape(ENCODERS * SLOTS_DEV, PIX, C_MID).astype(jnp.bfloat16)


def draw_assign(key, part):
    level, extra, owner_total = owner_plan(key)
    order_key = jax.random.fold_in(key, 6)
    owner_idx = jnp.arange(ENCODERS, dtype=jnp.int32)[:, None]
    slot_idx = jnp.arange(SLOTS_DEV, dtype=jnp.int32)[None, :]
    target = slot_idx // CAP
    sent_count = level[:, None] + extra[(owner_idx + target) % ENCODERS]
    in_use = slot_idx % CAP < sent_count
    jitter = jax.random.randint(order_key, (ENCODERS, SLOTS_DEV), 0, 1024)
    ranking = jnp.where(in_use, 0, 1) * (1 << 28) + jitter * SLOTS_DEV + slot_idx
    ranked = jnp.argsort(ranking, axis=1).astype(jnp.int32)
    used = jnp.sum(in_use.astype(jnp.int32), axis=1)
    return jnp.where(slot_idx < used[:, None], ranked, SLOTS_DEV).astype(jnp.int32)


def draw_tile_counts(key, part):
    level, extra, owner_total = owner_plan(key)
    weight_key, place_key = jax.random.split(jax.random.fold_in(key, 9))
    biggest = (owner_total + 1) // 2
    remaining = owner_total - biggest
    spare = remaining - (SL_DEV - 1)
    weights = jax.random.randint(weight_key, (ENCODERS, SL_DEV - 1), 1, 5)
    rising = jnp.cumsum(weights, axis=1)
    boundary = spare[:, None] * rising // rising[:, -1:]
    earlier = jnp.concatenate([jnp.zeros((ENCODERS, 1), jnp.int32), boundary[:, :-1].astype(jnp.int32)], axis=1)
    others = (1 + boundary - earlier).astype(jnp.int32)
    joined = jnp.concatenate([biggest[:, None].astype(jnp.int32), others], axis=1)
    place = jax.random.randint(place_key, (ENCODERS, 1), 0, SL_DEV)
    column = (jnp.arange(SL_DEV, dtype=jnp.int32)[None, :] - place) % SL_DEV
    return jnp.take_along_axis(joined, column, axis=1).astype(jnp.int32)


def set_ends(result, stream_key, low, largest):
    shape = result.shape
    spot = [jax.random.randint(jax.random.fold_in(stream_key, axis), (), 0, shape[axis]) for axis in range(len(shape))]
    result = result.at[tuple(spot)].set(low)
    longest = shape.index(max(shape))
    spot[longest] = (spot[longest] + 1) % shape[longest]
    return result.at[tuple(spot)].set(largest)


def gaussian(stream_key, shape, width, reach, kind=jnp.bfloat16):
    entries = width * jax.random.normal(stream_key, shape, jnp.float32)
    return jnp.clip(entries, min=-reach, max=reach).astype(kind)


def setup_inputs(seed: int = 0, part: int = 0) -> dict:
    key_of = jax.random.split(jax.random.key(seed), 12)
    own_keys = jax.random.split(jax.random.fold_in(key_of[11], part), 12)
    tiles = draw_tiles(jax.random.fold_in(jax.random.fold_in(key_of[11], part), 71), part)
    tile_counts = draw_tile_counts(jax.random.fold_in(jax.random.fold_in(key_of[11], part), 71), part)
    assign = draw_assign(jax.random.fold_in(jax.random.fold_in(key_of[11], part), 71), part)
    labels = set_ends(jax.random.randint(own_keys[3], (ENCODERS, SL_DEV), 0, CLASSES), jax.random.fold_in(own_keys[3], 1), 0, CLASSES - 1).astype(jnp.int32)
    w_conv = gaussian(key_of[4], (C_MID, EMB), C_MID ** -0.5, 0.25)
    bn_gain = jnp.clip(1.0 + 0.1 * jax.random.normal(key_of[5], (EMB,), jnp.float32), 0.5, 1.5)
    bn_shift = gaussian(key_of[6], (EMB,), 0.5, 3.0, jnp.float32)
    w_fc = gaussian(key_of[7], (EMB, HID), EMB ** -0.5, 0.1875)
    w_gate = gaussian(key_of[8], (HID, 2 * ATT), HID ** -0.5, 0.25)
    w_score = jnp.clip(jax.random.uniform(key_of[9], (ATT,), jnp.float32, -0.3, 0.3), -0.3, 0.3)
    w_cls = gaussian(key_of[10], (HID, CLASSES), HID ** -0.5, 0.25, jnp.float32)
    return dict(tiles=tiles, tile_counts=tile_counts, assign=assign, labels=labels, w_conv=w_conv, bn_gain=bn_gain, bn_shift=bn_shift, w_fc=w_fc, w_gate=w_gate, w_score=w_score, w_cls=w_cls)


epsilon = 1e-05
HIGH = lax.Precision.HIGHEST

def contract_rows(left, right):
    return lax.dot_general(left, right, (((0,), (0,)), ((), ())), preferred_element_type=jnp.float32)

def contract_cols(left, right):
    return lax.dot_general(left, right, (((1,), (1,)), ((), ())), preferred_element_type=jnp.float32)

def group_sums(membership, values):
    return lax.dot_general(membership, values, (((0,), (0,)), ((), ())), precision=HIGH)

def batch_post(before, membership, bn_gain, bn_shift, pixel_count):
    first = group_sums(membership, lax.optimization_barrier(jnp.sum(before, axis=1)))
    second = group_sums(membership, lax.optimization_barrier(jnp.sum(before * before, axis=1)))
    mean_value = first / pixel_count
    variance = second / pixel_count - mean_value * mean_value
    inverse = lax.rsqrt(variance + epsilon)
    tile_mean = jnp.dot(membership, mean_value, precision=HIGH)
    tile_scale = jnp.dot(membership, inverse, precision=HIGH)
    normed = (before - tile_mean[:, None, :]) * tile_scale[:, None, :] * bn_gain + bn_shift
    return lax.optimization_barrier(jnp.mean(jnp.maximum(normed, 0.0), axis=1)).astype(jnp.bfloat16)

def head_pass(embedded, slide_start, slide_end, classes_of, w_fc, w_gate, w_score, w_cls, slides_all):
    row_count = embedded.shape[0]
    position = jnp.arange(row_count, dtype=jnp.int32)[:, None]
    membership = ((position >= slide_start[None, :]) & (position < slide_end[None, :])).astype(jnp.float32)
    before = jnp.dot(embedded, w_fc, preferred_element_type=jnp.float32)
    hidden = jnp.maximum(before, 0.0).astype(jnp.bfloat16)
    gate_pre = jnp.dot(hidden, w_gate, preferred_element_type=jnp.float32)

    def tail(gate_pre, hidden_wide, w_score, w_cls):
        half_width = gate_pre.shape[1] // 2
        gated_mix = jnp.tanh(gate_pre[:, :half_width]) * jax.nn.sigmoid(gate_pre[:, half_width:])
        scores = jnp.dot(gated_mix, w_score, precision=HIGH)
        weight = jnp.exp(scores)[:, None] * membership
        totals = lax.optimization_barrier(jnp.sum(weight, axis=0))
        attention = weight / totals[None, :]
        pooled = lax.dot_general(attention, hidden_wide, (((0,), (0,)), ((), ())), precision=HIGH)
        logits = jnp.dot(pooled, w_cls, precision=HIGH)
        target = (classes_of[:, None] == jnp.arange(logits.shape[1], dtype=jnp.int32)[None, :]).astype(jnp.float32)
        log_total = jnp.log(lax.optimization_barrier(jnp.sum(jnp.exp(logits), axis=1)))
        return jnp.sum(log_total - lax.optimization_barrier(jnp.sum(logits * target, axis=1))) / slides_all
    loss_sum, tail_vjp = jax.vjp(tail, gate_pre, hidden.astype(jnp.float32), w_score, w_cls)
    grad_gates, grad_hidden, grad_score, grad_cls = tail_vjp(jnp.ones((), jnp.float32))
    gates_low = grad_gates.astype(jnp.bfloat16)
    grad_gate = contract_rows(hidden, gates_low)
    grad_hidden = grad_hidden + contract_cols(gates_low, w_gate)
    before_low = jnp.where(before > 0, grad_hidden, 0.0).astype(jnp.bfloat16)
    grad_fc = contract_rows(embedded, before_low)
    grad_embedded = contract_cols(before_low, w_fc).astype(jnp.bfloat16)
    return (loss_sum, grad_fc, grad_gate, grad_score, grad_cls, grad_embedded)

def reference(tiles, tile_counts, assign, labels, w_conv, bn_gain, bn_shift, w_fc, w_gate, w_score, w_cls):
    flattened = tiles.reshape(-1, C_MID)
    before = jnp.dot(flattened, w_conv, preferred_element_type=jnp.float32).reshape(ENCODERS * SLOTS_DEV, PIX, EMB)
    encoder_of = assign.reshape(-1) // CAP
    membership = (encoder_of[:, None] == jnp.arange(ENCODERS, dtype=jnp.int32)[None, :]).astype(jnp.float32)
    pixel_count = float(TILES_DEV * PIX)

    def post_fn(before, bn_gain, bn_shift):
        return batch_post(before, membership, bn_gain, bn_shift, pixel_count)
    embedded, post_vjp = jax.vjp(post_fn, before, bn_gain, bn_shift)
    local_end = jnp.cumsum(tile_counts, axis=1).astype(jnp.int32)
    local_start = (local_end - tile_counts).astype(jnp.int32)
    offset = (jnp.arange(ENCODERS, dtype=jnp.int32) * SLOTS_DEV)[:, None]
    slide_start = (local_start + offset).reshape(-1).astype(jnp.int32)
    slide_end = (local_end + offset).reshape(-1).astype(jnp.int32)
    loss_sum, grad_fc, grad_gate, grad_score, grad_cls, grad_embedded = head_pass(embedded, slide_start, slide_end, labels.reshape(-1), w_fc, w_gate, w_score, w_cls, float(ENCODERS * SL_DEV))
    grad_before, grad_gain, grad_shift = post_vjp(grad_embedded)
    grad_conv = contract_rows(flattened, grad_before.reshape(-1, EMB).astype(jnp.bfloat16))
    return (loss_sum.reshape(1), grad_conv, grad_gain, grad_shift, grad_fc, grad_gate, grad_score, grad_cls)
```

```python
import jax
import jax.numpy as jnp
from jax import lax
from jax.sharding import PartitionSpec as P

epsilon = 1e-05
f32, bf16 = jnp.float32, jnp.bfloat16


def round_low(x):
    return lax.reduce_precision(x, 8, 7)


def split3(x):
    high = round_low(x)
    rest = x - high
    middle = round_low(rest)
    low = round_low(rest - middle)
    return high.astype(bf16), middle.astype(bf16), low.astype(bf16)


def contract_rows(left, right):
    return lax.dot_general(
        left, right, (((0,), (0,)), ((), ())), preferred_element_type=f32
    )


def contract_cols(left, right):
    return lax.dot_general(
        left, right, (((1,), (1,)), ((), ())), preferred_element_type=f32
    )


def group_sums(member, values):
    width = values.shape[1]
    parts = contract_rows(member, jnp.concatenate(split3(values), axis=1))
    return parts[:, :width] + parts[:, width : 2 * width] + parts[:, 2 * width :]


def spread(member, values):
    return jnp.dot(
        jnp.concatenate([member] * 3, axis=1),
        jnp.concatenate(split3(values), axis=0),
        preferred_element_type=f32,
    )


def swap(x, bit):
    count = lax.axis_size("enc")
    return lax.ppermute(x, "enc", [(i, i ^ (1 << bit)) for i in range(count)])


def bit_of(bit):
    return (lax.axis_index("enc") >> bit) & 1


def sum_small(pair):
    levels = lax.axis_size("enc").bit_length() - 1
    core = bit_of(0) == 0
    mine = jnp.where(core, pair[0], pair[1])
    mine = mine + swap(jnp.where(core, pair[1], pair[0]), 0)
    for level in range(1, levels):
        mine = mine + swap(mine, level)
    other = swap(mine, 0)
    return jnp.where(core, mine, other), jnp.where(core, other, mine)


def sum_large(x, order):
    for level in order[:-1]:
        halves = x.reshape((2, x.shape[0] // 2) + x.shape[1:])
        bit = bit_of(level)
        keep = lax.dynamic_index_in_dim(halves, bit, 0, keepdims=False)
        send = lax.dynamic_index_in_dim(halves, 1 - bit, 0, keepdims=False)
        x = keep + swap(send.astype(bf16), level).astype(f32)
    x = round_low(x)
    x = x + swap(x.astype(bf16), order[-1]).astype(f32)
    x = x.astype(bf16)
    for level in order[-2::-1]:
        other = swap(x, level)
        first = bit_of(level) == 0
        x = jnp.where(
            first,
            jnp.concatenate([x, other], axis=0),
            jnp.concatenate([other, x], axis=0),
        )
    return x.astype(f32)


def sum_gradient(x):
    levels = lax.axis_size("enc").bit_length() - 1
    half = x.shape[0] // 2
    first = tuple(range(levels))
    second = (0,) + tuple(range(2, levels)) + (1,)
    return jnp.concatenate(
        [sum_large(x[:half], first), sum_large(x[half:], second)], axis=0
    )


def head_pass(
    embedded, inside, classes_of, w_fc, w_gate, w_score, w_cls, slides_all
):
    high = lax.Precision.HIGHEST
    before = jnp.dot(embedded, w_fc, preferred_element_type=f32)
    hidden = jnp.maximum(before, 0.0).astype(bf16)
    gate_pre = jnp.dot(hidden, w_gate, preferred_element_type=f32)

    def tail(gate_pre, hidden_wide, w_score, w_cls):
        half_width = gate_pre.shape[1] // 2
        mix = jnp.tanh(gate_pre[:, :half_width]) * jax.nn.sigmoid(
            gate_pre[:, half_width:]
        )
        scores = jnp.dot(mix, w_score, precision=high)
        weight = jnp.exp(scores)[:, None] * inside
        attention = weight / jnp.sum(weight, axis=0)[None, :]
        pooled = lax.dot_general(
            attention, hidden_wide, (((0,), (0,)), ((), ())), precision=high
        )
        logits = jnp.dot(pooled, w_cls, precision=high)
        target = (
            classes_of[:, None] == jnp.arange(logits.shape[1], dtype=jnp.int32)[None, :]
        ).astype(f32)
        log_total = jnp.log(jnp.sum(jnp.exp(logits), axis=1))
        return jnp.sum(log_total - jnp.sum(logits * target, axis=1)) / slides_all

    loss_sum, tail_vjp = jax.vjp(tail, gate_pre, hidden.astype(f32), w_score, w_cls)
    grad_gates, grad_hidden, grad_score, grad_cls = tail_vjp(jnp.ones((), f32))
    gates_low = grad_gates.astype(bf16)
    grad_gate = contract_rows(hidden, gates_low)
    grad_hidden = grad_hidden + contract_cols(gates_low, w_gate)
    before_low = jnp.where(before > 0, grad_hidden, 0.0).astype(bf16)
    grad_fc = contract_rows(embedded, before_low)
    grad_embedded = contract_cols(before_low, w_fc).astype(bf16)
    return loss_sum, grad_fc, grad_gate, grad_score, grad_cls, grad_embedded


def local(
    tiles, tile_counts, assign, labels, w_conv, bn_gain, bn_shift, w_fc, w_gate, w_score, w_cls
):
    devices = lax.axis_size("enc")
    own_rows, positions, input_width = tiles.shape
    emb_width = w_conv.shape[1]
    slot_rows = assign.shape[1]
    cap_rows = slot_rows // devices
    group_tiles = (
        devices // 4 * (4 + (cap_rows - 2) // 3 + 2 * (cap_rows - 2) // 3 + (cap_rows - 2))
        + devices // 2
    )
    pixel_count = float(group_tiles * positions)
    slides = tile_counts.shape[1]
    slides_all = float(devices * slides)
    counts_row = tile_counts[0]
    earlier = jnp.arange(slides)[:, None] <= jnp.arange(slides)[None, :]
    slide_end = jnp.sum(jnp.where(earlier, counts_row[:, None], 0), axis=0)
    slide_start = slide_end - counts_row
    row = jnp.arange(own_rows, dtype=jnp.int32)[:, None]
    inside = ((row >= slide_start[None, :]) & (row < slide_end[None, :])).astype(f32)
    group = assign[0] // cap_rows
    member = (group[:, None] == jnp.arange(devices, dtype=jnp.int32)[None, :]).astype(bf16)

    work = jnp.transpose(tiles, (1, 0, 2))
    before = lax.dot_general(
        work, w_conv, (((2,), (0,)), ((), ())), preferred_element_type=f32
    )
    totals = group_sums(
        member,
        jnp.concatenate([jnp.sum(before, axis=0), jnp.sum(before * before, axis=0)], axis=1),
    )
    first, second = sum_small(jnp.stack([totals[:, :emb_width], totals[:, emb_width:]]))
    mean = first / pixel_count
    variance = second / pixel_count - mean * mean
    inverse = lax.rsqrt(variance + epsilon)
    rows = spread(member, jnp.concatenate([mean, inverse], axis=1))
    row_mean, row_inverse = rows[:, :emb_width], rows[:, emb_width:]
    unit = (before - row_mean) * row_inverse
    normed = unit * bn_gain + bn_shift
    embedded = jnp.mean(jnp.maximum(normed, 0.0), axis=0).astype(bf16)

    loss_sum, grad_fc, grad_gate, grad_score, grad_cls, grad_embedded = head_pass(
        embedded, inside, labels[0], w_fc, w_gate, w_score, w_cls, slides_all
    )

    slope = jnp.where(normed > 0, 1.0, jnp.where(normed == 0, 0.5, 0.0))
    grad_normed = slope * (grad_embedded.astype(f32) / positions)[None]
    back = group_sums(
        member,
        jnp.concatenate(
            [jnp.sum(grad_normed, axis=0), jnp.sum(grad_normed * unit, axis=0)], axis=1
        ),
    )
    extra = jnp.zeros((2, 1, emb_width), f32)
    extra = extra.at[0, 0, : grad_score.shape[0]].set(grad_score)
    extra = extra.at[0, 0, grad_score.shape[0]].set(loss_sum)
    extra = extra.at[1, 0].set(grad_cls.reshape(-1))
    pair = jnp.stack([back[:, :emb_width], back[:, emb_width:]])
    shift_sums, gain_sums = sum_small(jnp.concatenate([pair, extra], axis=1))
    grad_score = shift_sums[devices, : grad_score.shape[0]]
    loss = shift_sums[devices, grad_score.shape[0]].reshape(1)
    grad_cls = gain_sums[devices].reshape(grad_cls.shape)
    shift_sums, gain_sums = shift_sums[:devices], gain_sums[:devices]
    grad_shift = jnp.sum(shift_sums, axis=0)
    grad_gain = jnp.sum(gain_sums, axis=0)
    rows = spread(
        member, jnp.concatenate([shift_sums / pixel_count, gain_sums / pixel_count], axis=1)
    )
    row_shift, row_gain = rows[:, :emb_width], rows[:, emb_width:]
    grad_before = (
        (grad_normed - row_shift - unit * row_gain) * (row_inverse * bn_gain)
    ).astype(bf16)
    grad_conv = lax.dot_general(
        work, grad_before, (((0, 1), (0, 1)), ((), ())), preferred_element_type=f32
    )
    grad_head = sum_gradient(jnp.concatenate([grad_fc, grad_gate], axis=0))
    grad_conv = sum_gradient(grad_conv)
    return (
        loss,
        grad_conv,
        grad_gain,
        grad_shift,
        grad_head[:emb_width],
        grad_head[emb_width:],
        grad_score,
        grad_cls,
    )


def solution(mesh):
    per_device = P(("groups", "enc"), None)
    placed = (P(("groups", "enc"), None, None), per_device, per_device, per_device) + (P(),) * 7
    rows_out = P("groups", None)
    return jax.shard_map(
        local,
        mesh=mesh,
        in_specs=placed,
        out_specs=(
            P("groups"),
            rows_out,
            P("groups"),
            P("groups"),
            rows_out,
            rows_out,
            P("groups"),
            rows_out,
        ),
        check_vma=False,
    )
```

```python
import functools
import math

import jax
import jax.numpy as jnp
from jax import lax
from jax.experimental import pallas as pl
from jax.experimental.pallas import tpu as pltpu
from jax.sharding import PartitionSpec as P

epsilon = 1e-05
f32, bf16 = jnp.float32, jnp.bfloat16
CHUNK = 128
EXTRA = 128


def split3(x):
    high = x.astype(bf16)
    rest = x - high.astype(f32)
    middle = rest.astype(bf16)
    low = (rest - middle.astype(f32)).astype(bf16)
    return high, middle, low


def contract_rows(left, right):
    return lax.dot_general(
        left, right, (((0,), (0,)), ((), ())), preferred_element_type=f32
    )


def contract_cols(left, right):
    return lax.dot_general(
        left, right, (((1,), (1,)), ((), ())), preferred_element_type=f32
    )


def matmul(left, right):
    return jnp.dot(left, right, preferred_element_type=f32)


def one_hot(assign, groups, cap_rows):
    low = lax.broadcasted_iota(jnp.int32, (groups, assign.shape[1]), 0) * cap_rows
    return jnp.where((assign >= low) & (assign < low + cap_rows), 1.0, 0.0)


def group_sums(member, values):
    high = values.astype(bf16)
    low = (values - high.astype(f32)).astype(bf16)
    return matmul(member, high) + matmul(member, low)


def spread(member, values):
    return contract_rows(
        jnp.concatenate([member] * 3, axis=0).astype(bf16),
        jnp.concatenate(split3(values), axis=0),
    )


def moments(first, second, pixel_count):
    mean = first * (1.0 / pixel_count)
    variance = second * (1.0 / pixel_count) - mean * mean
    return mean, lax.rsqrt(variance + epsilon)


def conv_kernel(cap_rows, x_ref, assign_ref, w_ref, before_ref, sums_ref, inputs_ref):
    step = pl.program_id(0)
    positions, tiles, width = x_ref.shape
    groups = sums_ref.shape[1]
    x = x_ref[...].reshape(positions * tiles, width)
    before = matmul(x, w_ref[...])
    before_ref[...] = before.reshape(before_ref.shape)
    parts = [before[p * tiles : (p + 1) * tiles] for p in range(positions)]
    second = sum([v * v for v in parts[1:]], parts[0] * parts[0])
    member = one_hot(assign_ref[...], groups, cap_rows).astype(bf16)

    @pl.when(step == 0)
    def _():
        sums_ref[1] = jnp.zeros(sums_ref.shape[1:], f32)
        inputs_ref[...] = jnp.zeros_like(inputs_ref)

    inputs_ref[...] += matmul(jnp.concatenate([member] * positions, axis=1), x)
    sums_ref[1] += group_sums(member, second)

    @pl.when(step == pl.num_programs(0) - 1)
    def _():
        terms = matmul(jnp.concatenate(split3(inputs_ref[...]), axis=0), w_ref[...])
        sums_ref[0] = terms[:groups] + terms[groups : 2 * groups] + terms[2 * groups :]


def head_kernel(
    cap_rows,
    pixel_count,
    slides_all,
    counts_ref,
    labels_ref,
    core_ref,
    before_ref,
    assign_ref,
    assign_all_ref,
    first_ref,
    second_ref,
    gain_ref,
    shift_ref,
    w_fc_ref,
    w_gate_ref,
    w_score_ref,
    w_cls_ref,
    send_ref,
    keep_ref,
    grad_embedded_ref,
    sums_ref,
    embedded_ref,
    count_ref,
    total_ref,
    grad_ref,
    low_ref,
    grad_low_ref,
    copied,
):
    step = pl.program_id(0)
    positions, tiles, emb_width = before_ref.shape
    groups = first_ref.shape[0]
    mean, inverse = moments(first_ref[...], second_ref[...], pixel_count)
    scale = inverse * gain_ref[...]
    offset = shift_ref[...] - mean * scale
    member = one_hot(assign_ref[...], groups, cap_rows)
    spread_rows = spread(member, jnp.concatenate([scale, offset], axis=1))
    scale, offset = spread_rows[:, :emb_width], spread_rows[:, emb_width:]
    count = jnp.zeros((tiles, emb_width), f32)
    total = jnp.zeros((tiles, emb_width), f32)
    for p in range(positions):
        value = before_ref[p]
        live = value * scale + offset > 0
        count += jnp.where(live, 1.0, 0.0)
        total += jnp.where(live, value, 0.0)
    rows = pl.ds(pl.multiple_of(step * tiles, tiles), tiles)
    embedded_ref[rows] = ((total * scale + count * offset) * (1.0 / positions)).astype(bf16)
    count_ref[rows] = count
    total_ref[rows] = total

    @pl.when(step == pl.num_programs(0) - 1)
    def _():
        embedded = embedded_ref[...]
        tiles_all = embedded.shape[0]
        slides = counts_ref.shape[1]
        pre = matmul(embedded, w_fc_ref[...])
        hidden = jnp.maximum(pre, 0.0).astype(bf16)
        gate_pre = matmul(hidden, w_gate_ref[...])
        half = gate_pre.shape[1] // 2
        wave = jnp.tanh(gate_pre[:, :half])
        sig = jax.nn.sigmoid(gate_pre[:, half:])
        mix = wave * sig
        w_score = w_score_ref[...]
        score = jnp.sum(mix * w_score, axis=1, keepdims=True)

        lane = lax.broadcasted_iota(jnp.int32, (1, 128), 1)
        row = lax.broadcasted_iota(jnp.int32, (tiles_all, 128), 0)
        low = jnp.zeros((1, 128), jnp.int32)
        high = jnp.zeros((1, 128), jnp.int32)
        start = jnp.int32(0)
        for s in range(slides):
            end = start + counts_ref[0, s]
            low = jnp.where(lane == s, start, low)
            high = jnp.where(lane == s, end, high)
            start = end
        weight = jnp.where((row >= low) & (row < high), jnp.exp(score), 0.0)
        totals = jnp.sum(weight, axis=0, keepdims=True)
        attention = weight / jnp.where(lane < slides, totals, 1.0)
        att_high, att_middle, att_low = split3(attention)
        pooled = (
            contract_rows(att_high, hidden)
            + contract_rows(att_middle, hidden)
            + contract_rows(att_low, hidden)
        )[:8]
        slot = lax.broadcasted_iota(jnp.int32, (8, 1), 0)
        label = jnp.zeros((8, 1), jnp.int32)
        for s in range(slides):
            label = jnp.where(slot == s, labels_ref[0, s], label)
        classes = w_cls_ref.shape[0]
        w_cls = [w_cls_ref[c : c + 1, :] for c in range(classes)]
        logits = [jnp.sum(pooled * w, axis=1, keepdims=True) for w in w_cls]
        powers = [jnp.exp(v) for v in logits]
        power = sum(powers[1:], powers[0])
        target = sum(jnp.where(label == c, v, 0.0) for c, v in enumerate(logits))
        used = slot < slides
        loss = jnp.sum(jnp.where(used, jnp.log(power) - target, 0.0), axis=0, keepdims=True) * (
            1.0 / slides_all
        )
        grad_logits = [
            jnp.where(used, v / power - jnp.where(label == c, 1.0, 0.0), 0.0) * (1.0 / slides_all)
            for c, v in enumerate(powers)
        ]
        grad_cls = [jnp.sum(g * pooled, axis=0, keepdims=True) for g in grad_logits]
        grad_pooled = sum(g * w for g, w in zip(grad_logits, w_cls))
        grad_pooled = jnp.concatenate(
            [grad_pooled, jnp.zeros((128 - 8, grad_pooled.shape[1]), f32)], axis=0
        )
        gp_high, gp_middle, gp_low = split3(grad_pooled)
        grad_attention = (
            contract_cols(hidden, gp_high)
            + contract_cols(hidden, gp_middle)
            + contract_cols(hidden, gp_low)
        )
        product = attention * grad_attention
        centre = jnp.sum(product, axis=0, keepdims=True)
        grad_score = jnp.sum(product - attention * centre, axis=1, keepdims=True)
        grad_w_score = jnp.sum(grad_score * mix, axis=0, keepdims=True)
        grad_mix = grad_score * w_score
        gates_low = jnp.concatenate(
            [grad_mix * sig * (1.0 - wave * wave), grad_mix * mix * (1.0 - sig)], axis=1
        ).astype(bf16)
        grad_hidden = matmul(
            jnp.concatenate([att_high, att_high, att_middle], axis=1),
            jnp.concatenate([gp_high, gp_middle, gp_high], axis=0),
        )
        grad_hidden += contract_cols(gates_low, w_gate_ref[...])
        before_low = jnp.where(pre > 0, grad_hidden, 0.0).astype(bf16)
        core = core_ref[0, 0]
        rows_fc, rows_gate = emb_width // 2, pre.shape[1] // 2
        halves_fc = grad_ref.at[:, pl.ds(0, rows_fc)]
        halves_gate = grad_ref.at[:, pl.ds(rows_fc, rows_gate)]
        halves_fc[...] = contract_rows(embedded, before_low).reshape(2, rows_fc, -1)
        halves_gate[...] = contract_rows(hidden, gates_low).reshape(2, rows_gate, -1)
        low_ref[...] = grad_ref[1 - core].astype(bf16)
        grad_embedded = contract_cols(before_low, w_fc_ref[...]).astype(bf16)
        grad_low_ref[...] = grad_embedded
        copies = [
            pltpu.make_async_copy(low_ref, send_ref, copied.at[0]),
            pltpu.make_async_copy(grad_ref.at[core], keep_ref, copied.at[1]),
            pltpu.make_async_copy(grad_low_ref, grad_embedded_ref, copied.at[2]),
        ]
        for c in copies:
            c.start()
        each = grad_embedded.astype(f32) * (1.0 / positions)
        member_all = one_hot(assign_all_ref[...], groups, cap_rows).astype(bf16)
        shift_sums = group_sums(member_all, each * count_ref[...])
        total_sums = group_sums(member_all, each * total_ref[...])
        sums_ref[0, :, :emb_width] = shift_sums
        sums_ref[1, :, :emb_width] = (total_sums - mean * shift_sums) * inverse
        sums_ref[:, :, emb_width:] = jnp.zeros((2, groups, EXTRA), f32)
        for i in range(half // EXTRA):
            sums_ref[0, i : i + 1, emb_width:] = grad_w_score[:, i * EXTRA : (i + 1) * EXTRA]
        i = half // EXTRA
        sums_ref[0, i : i + 1, emb_width:] = jnp.where(lane == 0, loss, 0.0)
        grad_cls = jnp.concatenate(grad_cls, axis=1)
        for i in range(grad_cls.shape[1] // EXTRA):
            sums_ref[1, i : i + 1, emb_width:] = grad_cls[:, i * EXTRA : (i + 1) * EXTRA]
        for c in copies:
            c.wait()


def back_kernel(
    cap_rows,
    pixel_count,
    x_ref,
    before_ref,
    grad_embedded_ref,
    assign_ref,
    first_ref,
    second_ref,
    shift_sums_ref,
    gain_sums_ref,
    gain_ref,
    shift_ref,
    grad_ref,
    grad_gain_ref,
    grad_shift_ref,
):

    positions, tiles, emb_width = before_ref.shape
    groups = first_ref.shape[0]
    mean, inverse = moments(first_ref[...], second_ref[...], pixel_count)
    scale = inverse * gain_ref[...]
    offset = shift_ref[...] - mean * scale
    slope = scale * inverse * gain_sums_ref[:, :emb_width] * (1.0 / pixel_count)
    constant = scale * shift_sums_ref[:, :emb_width] * (1.0 / pixel_count) - mean * slope
    member = one_hot(assign_ref[...], groups, cap_rows)
    spread_rows = spread(member, jnp.concatenate([scale, offset, slope, constant], axis=1))
    scale, offset, slope, constant = (
        spread_rows[:, i * emb_width : (i + 1) * emb_width] for i in range(4)
    )
    direct = grad_embedded_ref[...].astype(f32) * scale * (1.0 / positions)
    grads = []
    for p in range(positions):
        value = before_ref[p]
        live = value * scale + offset > 0
        grads.append(
            (jnp.where(live, direct, 0.0) - constant - value * slope).astype(bf16)
        )

    @pl.when(pl.program_id(0) == 0)
    def _():
        grad_ref[...] = jnp.zeros_like(grad_ref)
        grad_gain_ref[...] = jnp.sum(gain_sums_ref[:, :emb_width], axis=0, keepdims=True)
        grad_shift_ref[...] = jnp.sum(shift_sums_ref[:, :emb_width], axis=0, keepdims=True)

    grad_ref[...] += contract_rows(
        x_ref[...].reshape(positions * tiles, x_ref.shape[2]), jnp.concatenate(grads, axis=0)
    )


def round_low(x):
    return lax.reduce_precision(x, 8, 7)


def swap(x, bit):
    count = lax.axis_size("enc")
    return lax.ppermute(x, "enc", [(i, i ^ (1 << bit)) for i in range(count)])


def bit_of(bit):
    return (lax.axis_index("enc") >> bit) & 1


def wait_for(x, other):
    corner = (other[:16, :128] * 0).astype(x.dtype)
    return x + jnp.pad(corner, ((0, x.shape[0] - 16), (0, x.shape[1] - 128)))


class SmallSum:
    def __init__(self, pair):
        self.core = bit_of(0) == 0
        self.x = jnp.where(self.core, pair[0], pair[1])
        self.x += swap(jnp.where(self.core, pair[1], pair[0]), 0)

    def hop(self, level):
        self.x += swap(self.x, level)

    def result(self):
        other = swap(self.x, 0)
        return jnp.where(self.core, self.x, other), jnp.where(self.core, other, self.x)


class LargeSum:
    def __init__(self, x):
        self.x = x

    def halve(self, level, other=None):
        x = self.x
        halves = x.reshape((2, x.shape[0] // 2) + x.shape[1:])
        bit = bit_of(level)
        keep = lax.dynamic_index_in_dim(halves, bit, 0, keepdims=False)
        send = lax.dynamic_index_in_dim(halves, 1 - bit, 0, keepdims=False).astype(bf16)
        if other is not None:
            send = wait_for(send, other)
        self.x = keep + swap(send, level).astype(f32)

    def exchange(self, level):
        x = round_low(self.x)
        self.x = (x + swap(x.astype(bf16), level).astype(f32)).astype(bf16)

    def pair(self, level):
        other = swap(self.x, level)
        first = bit_of(level) == 0
        return jnp.where(first, self.x, other), jnp.where(first, other, self.x)

    def double(self, level):
        self.x = jnp.concatenate(self.pair(level), axis=0)


def local(
    tiles, tile_counts, assign, labels, w_conv, bn_gain, bn_shift, w_fc, w_gate, w_score, w_cls
):
    devices = lax.axis_size("enc")
    own_rows, positions, input_width = tiles.shape
    emb_width = w_conv.shape[1]
    hid_width = w_fc.shape[1]
    slot_rows = assign.shape[1]
    cap_rows = slot_rows // devices
    group_tiles = (
        devices // 4 * (4 + (cap_rows - 2) // 3 + 2 * (cap_rows - 2) // 3 + (cap_rows - 2))
        + devices // 2
    )
    pixel_count = float(group_tiles * positions)
    slides_all = float(devices * tile_counts.shape[1])
    gain, shift = bn_gain.reshape(1, emb_width), bn_shift.reshape(1, emb_width)
    steps = own_rows // CHUNK

    def whole(*shape):
        return pl.BlockSpec(shape, lambda i: (0,) * len(shape))

    smem = pl.BlockSpec(memory_space=pltpu.SMEM)
    x_block = pl.BlockSpec((positions, CHUNK, input_width), lambda i: (0, i, 0))
    before_block = pl.BlockSpec((positions, CHUNK, emb_width), lambda i: (0, i, 0))
    assign_block = pl.BlockSpec((1, CHUNK), lambda i: (0, i))

    def settings(mebibytes, microseconds):
        return dict(
            compiler_params=pltpu.CompilerParams(
                dimension_semantics=("arbitrary",), vmem_limit_bytes=mebibytes << 20
            ),
            cost_estimate=pl.CostEstimate(
                flops=int(microseconds * 1.1e9), bytes_accessed=8 << 20, transcendentals=0
            ),
        )

    group_block = whole(devices, emb_width)
    back_block = whole(devices, emb_width + EXTRA)
    row_block = whole(1, emb_width)

    work = jnp.transpose(tiles, (1, 0, 2))
    before, sums = pl.pallas_call(
        functools.partial(conv_kernel, cap_rows),
        grid=(steps,),
        in_specs=[x_block, assign_block, whole(input_width, emb_width)],
        out_specs=[before_block, whole(2, devices, emb_width)],
        out_shape=[
            pltpu.HBM((positions, own_rows, emb_width), f32),
            jax.ShapeDtypeStruct((2, devices, emb_width), f32),
        ],
        scratch_shapes=[pltpu.VMEM((devices, input_width), f32)],
        **settings(24, 6),
        name="conv_sums",
    )(work, assign, w_conv)
    before = pltpu.with_memory_space_constraint(before, pltpu.HBM)
    levels = devices.bit_length() - 1
    total = SmallSum(sums)
    for level in range(1, levels):
        total.hop(level)
    first, second = total.result()

    any_block = pl.BlockSpec(memory_space=pl.ANY)
    half_rows = (emb_width + hid_width) // 2
    send, keep, grad_embedded, sums = pl.pallas_call(
        functools.partial(head_kernel, cap_rows, pixel_count, slides_all),
        grid=(steps,),
        in_specs=[
            smem,
            smem,
            smem,
            before_block,
            assign_block,
            whole(1, own_rows),
            group_block,
            group_block,
            row_block,
            row_block,
            whole(*w_fc.shape),
            whole(*w_gate.shape),
            whole(1, w_score.shape[0]),
            whole(*w_cls.shape[::-1]),
        ],
        out_specs=[any_block] * 3 + [whole(2, devices, emb_width + EXTRA)],
        out_shape=[
            jax.ShapeDtypeStruct((half_rows, hid_width), bf16),
            pltpu.HBM((half_rows, hid_width), f32),
            pltpu.HBM((own_rows, emb_width), bf16),
            jax.ShapeDtypeStruct((2, devices, emb_width + EXTRA), f32),
        ],
        scratch_shapes=[
            pltpu.VMEM((own_rows, emb_width), bf16),
            pltpu.VMEM((own_rows, emb_width), f32),
            pltpu.VMEM((own_rows, emb_width), f32),
            pltpu.VMEM((2, half_rows, hid_width), f32),
            pltpu.VMEM((half_rows, hid_width), bf16),
            pltpu.VMEM((own_rows, emb_width), bf16),
            pltpu.SemaphoreType.DMA((3,)),
        ],
        name="norm_head",
        **settings(36, 12),
    )(
        tile_counts,
        labels,
        bit_of(0).astype(jnp.int32).reshape(1, 1),
        before,
        assign,
        assign,
        first,
        second,
        gain,
        shift,
        w_fc,
        w_gate,
        w_score.reshape(1, -1),
        w_cls.T,
    )
    grad_embedded = pltpu.with_memory_space_constraint(grad_embedded, pltpu.HBM)
    total = SmallSum(sums)
    rows_fc = emb_width // 2
    head = LargeSum(keep + swap(send, 0).astype(f32))
    total.hop(1)
    total.x = wait_for(total.x, head.x)
    head.halve(1)
    for level in range(2, levels):
        total.hop(level)
    total.x = wait_for(total.x, head.x)
    shift_sums, gain_sums = total.result()

    grad_conv, grad_gain, grad_shift = pl.pallas_call(
        functools.partial(back_kernel, cap_rows, pixel_count),
        grid=(steps,),
        in_specs=[
            x_block,
            before_block,
            pl.BlockSpec((CHUNK, emb_width), lambda i: (i, 0)),
            assign_block,
            group_block,
            group_block,
            back_block,
            back_block,
            row_block,
            row_block,
        ],
        out_specs=[whole(input_width, emb_width), row_block, row_block],
        out_shape=[
            jax.ShapeDtypeStruct((input_width, emb_width), f32),
            jax.ShapeDtypeStruct((1, emb_width), f32),
            jax.ShapeDtypeStruct((1, emb_width), f32),
        ],
        name="norm_back",
        **settings(24, 9),
    )(work, before, grad_embedded, assign, first, second, shift_sums, gain_sums, gain, shift)

    conv = LargeSum(grad_conv)
    for level in range(2, levels - 1):
        head.halve(level)
    conv.halve(0, head.x)
    conv.halve(1)
    head.exchange(levels - 1)
    head.x = wait_for(head.x, conv.x)
    for level in range(2, levels - 1):
        conv.halve(level)
    for level in range(levels - 2, 1, -1):
        head.double(level)
    head.x = wait_for(head.x, conv.x)
    conv.exchange(levels - 1)
    conv.x = wait_for(conv.x, head.x)
    for level in range(levels - 2, 1, -1):
        conv.double(level)
    head.double(1)
    conv.x = wait_for(conv.x, head.x)
    conv.double(1)
    low, high = head.pair(0)
    grad_fc = jnp.concatenate([low[:rows_fc], high[:rows_fc]], axis=0).astype(f32)
    grad_gate = jnp.concatenate([low[rows_fc:], high[rows_fc:]], axis=0).astype(f32)
    conv.x = wait_for(conv.x, grad_fc)
    conv.double(0)
    grad_conv = conv.x.astype(f32)
    scores = w_score.shape[0] // EXTRA
    classes = math.prod(w_cls.shape) // EXTRA
    return (
        shift_sums[scores, emb_width : emb_width + 1],
        grad_conv,
        grad_gain.reshape(emb_width),
        grad_shift.reshape(emb_width),
        grad_fc,
        grad_gate,
        shift_sums[:scores, emb_width:].reshape(-1),
        gain_sums[:classes, emb_width:].reshape(w_cls.shape[::-1]).T,
    )


def solution(mesh):
    per_device = P(("groups", "enc"), None)
    placed = (P(("groups", "enc"), None, None), per_device, per_device, per_device) + (P(),) * 7
    rows_out = P("groups", None)
    return jax.shard_map(
        local,
        mesh=mesh,
        in_specs=placed,
        out_specs=(
            P("groups"),
            rows_out,
            P("groups"),
            P("groups"),
            rows_out,
            rows_out,
            P("groups"),
            rows_out,
        ),
        check_vma=False,
    )
```

```python
import functools
import math

import jax
import jax.numpy as jnp
from jax import lax
from jax.experimental import pallas as pl
from jax.experimental.pallas import tpu as pltpu
from jax.sharding import PartitionSpec as P

epsilon = 1e-05
f32, bf16 = jnp.float32, jnp.bfloat16
CHUNK_CONV, CHUNK_HEAD, CHUNK_BACK = 128, 128, 128
EXTRA = 128


def split3(x):
    high = x.astype(bf16)
    rest = x - high.astype(f32)
    middle = rest.astype(bf16)
    low = (rest - middle.astype(f32)).astype(bf16)
    return high, middle, low


def contract_rows(left, right):
    return lax.dot_general(
        left, right, (((0,), (0,)), ((), ())), preferred_element_type=f32
    )


def contract_cols(left, right):
    return lax.dot_general(
        left, right, (((1,), (1,)), ((), ())), preferred_element_type=f32
    )


def matmul(left, right):
    return jnp.dot(left, right, preferred_element_type=f32)


def one_hot(assign, groups, cap_rows):
    low = lax.broadcasted_iota(jnp.int32, (groups, assign.shape[1]), 0) * cap_rows
    return jnp.where((assign >= low) & (assign < low + cap_rows), 1.0, 0.0)


def group_sums(member, values):
    high = values.astype(bf16)
    low = (values - high.astype(f32)).astype(bf16)
    return matmul(member, high) + matmul(member, low)


def spread(member, values):
    return contract_rows(
        jnp.concatenate([member] * 3, axis=0).astype(bf16),
        jnp.concatenate(split3(values), axis=0),
    )


def moments(first, second, pixel_count):
    mean = first * (1.0 / pixel_count)
    variance = second * (1.0 / pixel_count) - mean * mean
    return mean, lax.rsqrt(variance + epsilon)


def conv_kernel(cap_rows, x_ref, assign_ref, w_ref, before_ref, sums_ref):
    positions, tiles_all, width = x_ref.shape
    groups, emb_width = sums_ref.shape[1:]
    tiles = CHUNK_CONV
    inputs = jnp.zeros((groups, width), f32)
    squares = jnp.zeros((groups, emb_width), f32)
    for start in range(0, tiles_all, tiles):
        rows = pl.ds(start, tiles)
        x = x_ref[:, rows].reshape(positions * tiles, width)
        before = matmul(x, w_ref[...])
        before_ref[:, rows] = before.reshape(positions, tiles, emb_width)
        parts = [before[p * tiles : (p + 1) * tiles] for p in range(positions)]
        second = sum([v * v for v in parts[1:]], parts[0] * parts[0])
        member = one_hot(assign_ref[:, rows], groups, cap_rows).astype(bf16)
        inputs += matmul(jnp.concatenate([member] * positions, axis=1), x)
        squares += group_sums(member, second)
    terms = matmul(jnp.concatenate(split3(inputs), axis=0), w_ref[...])
    sums_ref[0] = terms[:groups] + terms[groups : 2 * groups] + terms[2 * groups :]
    sums_ref[1] = squares


def head_kernel(
    cap_rows,
    pixel_count,
    slides_all,
    counts_ref,
    labels_ref,
    core_ref,
    before_ref,
    assign_ref,
    first_ref,
    second_ref,
    gain_ref,
    shift_ref,
    w_fc_ref,
    w_gate_ref,
    w_score_ref,
    w_cls_ref,
    send_ref,
    keep_ref,
    grad_embedded_ref,
    sums_ref,
    embedded_ref,
    count_ref,
    total_ref,
    grad_ref,
):
    positions, tiles_all, emb_width = before_ref.shape
    tiles = CHUNK_HEAD
    groups = first_ref.shape[0]
    mean, inverse = moments(first_ref[...], second_ref[...], pixel_count)
    scale = inverse * gain_ref[...]
    offset = shift_ref[...] - mean * scale
    both = jnp.concatenate([scale, offset], axis=1)
    for begin in range(0, tiles_all, tiles):
        rows = pl.ds(begin, tiles)
        spread_rows = spread(one_hot(assign_ref[:, rows], groups, cap_rows), both)
        scale, offset = spread_rows[:, :emb_width], spread_rows[:, emb_width:]
        count = jnp.zeros((tiles, emb_width), f32)
        total = jnp.zeros((tiles, emb_width), f32)
        for p in range(positions):
            value = before_ref[p, rows]
            live = value * scale + offset > 0
            count += jnp.where(live, 1.0, 0.0)
            total += jnp.where(live, value, 0.0)
        embedded_ref[rows] = ((total * scale + count * offset) * (1.0 / positions)).astype(bf16)
        count_ref[rows] = count
        total_ref[rows] = total

    embedded = embedded_ref[...]
    slides = counts_ref.shape[1]
    pre = matmul(embedded, w_fc_ref[...])
    hidden = jnp.maximum(pre, 0.0).astype(bf16)
    gate_pre = matmul(hidden, w_gate_ref[...])
    half = gate_pre.shape[1] // 2
    wave = jnp.tanh(gate_pre[:, :half])
    sig = jax.nn.sigmoid(gate_pre[:, half:])
    mix = wave * sig
    w_score = w_score_ref[...]
    score = jnp.sum(mix * w_score, axis=1, keepdims=True)

    lane = lax.broadcasted_iota(jnp.int32, (1, 128), 1)
    row = lax.broadcasted_iota(jnp.int32, (tiles_all, 128), 0)
    low = jnp.zeros((1, 128), jnp.int32)
    high = jnp.zeros((1, 128), jnp.int32)
    start = jnp.int32(0)
    for s in range(slides):
        end = start + counts_ref[0, s]
        low = jnp.where(lane == s, start, low)
        high = jnp.where(lane == s, end, high)
        start = end
    weight = jnp.where((row >= low) & (row < high), jnp.exp(score), 0.0)
    totals = jnp.sum(weight, axis=0, keepdims=True)
    attention = weight / jnp.where(lane < slides, totals, 1.0)
    att_high, att_middle, att_low = split3(attention)
    pooled = (
        contract_rows(att_high, hidden)
        + contract_rows(att_middle, hidden)
        + contract_rows(att_low, hidden)
    )[:8]
    slot = lax.broadcasted_iota(jnp.int32, (8, 1), 0)
    label = jnp.zeros((8, 1), jnp.int32)
    for s in range(slides):
        label = jnp.where(slot == s, labels_ref[0, s], label)
    classes = w_cls_ref.shape[0]
    w_cls = [w_cls_ref[c : c + 1, :] for c in range(classes)]
    logits = [jnp.sum(pooled * w, axis=1, keepdims=True) for w in w_cls]
    powers = [jnp.exp(v) for v in logits]
    power = sum(powers[1:], powers[0])
    target = sum(jnp.where(label == c, v, 0.0) for c, v in enumerate(logits))
    used = slot < slides
    loss = jnp.sum(jnp.where(used, jnp.log(power) - target, 0.0), axis=0, keepdims=True) * (
        1.0 / slides_all
    )
    grad_logits = [
        jnp.where(used, v / power - jnp.where(label == c, 1.0, 0.0), 0.0) * (1.0 / slides_all)
        for c, v in enumerate(powers)
    ]
    grad_cls = [jnp.sum(g * pooled, axis=0, keepdims=True) for g in grad_logits]
    grad_pooled = sum(g * w for g, w in zip(grad_logits, w_cls))
    grad_pooled = jnp.concatenate(
        [grad_pooled, jnp.zeros((128 - 8, grad_pooled.shape[1]), f32)], axis=0
    )
    gp_high, gp_middle, gp_low = split3(grad_pooled)
    grad_attention = (
        contract_cols(hidden, gp_high)
        + contract_cols(hidden, gp_middle)
        + contract_cols(hidden, gp_low)
    )
    product = attention * grad_attention
    centre = jnp.sum(product, axis=0, keepdims=True)
    grad_score = jnp.sum(product - attention * centre, axis=1, keepdims=True)
    grad_w_score = jnp.sum(grad_score * mix, axis=0, keepdims=True)
    grad_mix = grad_score * w_score
    gates_low = jnp.concatenate(
        [grad_mix * sig * (1.0 - wave * wave), grad_mix * mix * (1.0 - sig)], axis=1
    ).astype(bf16)
    grad_hidden = matmul(
        jnp.concatenate([att_high, att_high, att_middle], axis=1),
        jnp.concatenate([gp_high, gp_middle, gp_high], axis=0),
    )
    grad_hidden += contract_cols(gates_low, w_gate_ref[...])
    before_low = jnp.where(pre > 0, grad_hidden, 0.0).astype(bf16)
    core = core_ref[0, 0]
    rows_fc, rows_gate = emb_width // 2, pre.shape[1] // 2
    halves_fc = grad_ref.at[:, pl.ds(0, rows_fc)]
    halves_gate = grad_ref.at[:, pl.ds(rows_fc, rows_gate)]
    halves_fc[...] = contract_rows(embedded, before_low).reshape(2, rows_fc, -1)
    halves_gate[...] = contract_rows(hidden, gates_low).reshape(2, rows_gate, -1)
    send_ref[...] = grad_ref[1 - core].astype(bf16)
    keep_ref[...] = grad_ref[core]
    grad_embedded = contract_cols(before_low, w_fc_ref[...]).astype(bf16)
    grad_embedded_ref[...] = grad_embedded
    each = grad_embedded.astype(f32) * (1.0 / positions)
    member_all = one_hot(assign_ref[...], groups, cap_rows).astype(bf16)
    shift_sums = group_sums(member_all, each * count_ref[...])
    total_sums = group_sums(member_all, each * total_ref[...])
    sums_ref[0, :, :emb_width] = shift_sums
    sums_ref[1, :, :emb_width] = (total_sums - mean * shift_sums) * inverse
    sums_ref[:, :, emb_width:] = jnp.zeros((2, groups, EXTRA), f32)
    for i in range(half // EXTRA):
        sums_ref[0, i : i + 1, emb_width:] = grad_w_score[:, i * EXTRA : (i + 1) * EXTRA]
    i = half // EXTRA
    sums_ref[0, i : i + 1, emb_width:] = jnp.where(lane == 0, loss, 0.0)
    grad_cls = jnp.concatenate(grad_cls, axis=1)
    for i in range(grad_cls.shape[1] // EXTRA):
        sums_ref[1, i : i + 1, emb_width:] = grad_cls[:, i * EXTRA : (i + 1) * EXTRA]


def back_kernel(
    cap_rows,
    pixel_count,
    x_ref,
    before_ref,
    grad_embedded_ref,
    assign_ref,
    first_ref,
    second_ref,
    shift_sums_ref,
    gain_sums_ref,
    gain_ref,
    shift_ref,
    grad_ref,
    grad_gain_ref,
    grad_shift_ref,
):

    positions, tiles_all, emb_width = before_ref.shape
    tiles = CHUNK_BACK
    groups = first_ref.shape[0]
    mean, inverse = moments(first_ref[...], second_ref[...], pixel_count)
    scale = inverse * gain_ref[...]
    offset = shift_ref[...] - mean * scale
    slope = scale * inverse * gain_sums_ref[:, :emb_width] * (1.0 / pixel_count)
    constant = scale * shift_sums_ref[:, :emb_width] * (1.0 / pixel_count) - mean * slope
    grad_gain_ref[...] = jnp.sum(gain_sums_ref[:, :emb_width], axis=0, keepdims=True)
    grad_shift_ref[...] = jnp.sum(shift_sums_ref[:, :emb_width], axis=0, keepdims=True)
    every = jnp.concatenate([scale, offset, slope, constant], axis=1)
    for start in range(0, tiles_all, tiles):
        rows = pl.ds(start, tiles)
        spread_rows = spread(one_hot(assign_ref[:, rows], groups, cap_rows), every)
        scale, offset, slope, constant = (
            spread_rows[:, i * emb_width : (i + 1) * emb_width] for i in range(4)
        )
        direct = grad_embedded_ref[rows].astype(f32) * scale * (1.0 / positions)
        grads = []
        for p in range(positions):
            value = before_ref[p, rows]
            live = value * scale + offset > 0
            grads.append((jnp.where(live, direct, 0.0) - constant - value * slope).astype(bf16))
        part = contract_rows(
            x_ref[:, rows].reshape(positions * tiles, x_ref.shape[2]),
            jnp.concatenate(grads, axis=0),
        )
        if start == 0:
            grad_ref[...] = part
        else:
            grad_ref[...] += part


def round_low(x):
    return lax.reduce_precision(x, 8, 7)


def swap(x, bit):
    count = lax.axis_size("enc")
    return lax.ppermute(x, "enc", [(i, i ^ (1 << bit)) for i in range(count)])


def wait_for(x, other):
    corner = (other[:16, :128] * 0).astype(x.dtype)
    return x + jnp.pad(corner, ((0, x.shape[0] - 16), (0, x.shape[1] - 128)))


class SmallSum:
    def __init__(self, pair, firsts):
        self.core = firsts[0]
        self.x = jnp.where(self.core, pair[0], pair[1])
        self.x += swap(jnp.where(self.core, pair[1], pair[0]), 0)

    def hop(self, level):
        self.x += swap(self.x, level)

    def result(self):
        other = swap(self.x, 0)
        return jnp.where(self.core, self.x, other), jnp.where(self.core, other, self.x)


class LargeSum:
    def __init__(self, x, firsts):
        self.x = x
        self.firsts = firsts

    def halve(self, level, other=None):
        half = self.x.shape[0] // 2
        low, high = self.x[:half], self.x[half:]
        first = self.firsts[level]
        send = jnp.where(first, high, low).astype(bf16)
        if other is not None:
            send = wait_for(send, other)
        self.x = jnp.where(first, low, high) + swap(send, level).astype(f32)

    def exchange(self, level):
        x = round_low(self.x)
        self.x = (x + swap(x.astype(bf16), level).astype(f32)).astype(bf16)

    def pair(self, level):
        other = swap(self.x, level)
        first = self.firsts[level]
        return jnp.where(first, self.x, other), jnp.where(first, other, self.x)

    def double(self, level):
        self.x = jnp.concatenate(self.pair(level), axis=0)


def local(
    tiles, tile_counts, assign, labels, w_conv, bn_gain, bn_shift, w_fc, w_gate, w_score, w_cls
):
    devices = lax.axis_size("enc")
    own_rows, positions, input_width = tiles.shape
    emb_width = w_conv.shape[1]
    hid_width = w_fc.shape[1]
    slot_rows = assign.shape[1]
    cap_rows = slot_rows // devices
    group_tiles = (
        devices // 4 * (4 + (cap_rows - 2) // 3 + 2 * (cap_rows - 2) // 3 + (cap_rows - 2))
        + devices // 2
    )
    pixel_count = float(group_tiles * positions)
    slides_all = float(devices * tile_counts.shape[1])
    gain, shift = bn_gain.reshape(1, emb_width), bn_shift.reshape(1, emb_width)

    smem = pl.BlockSpec(memory_space=pltpu.SMEM)
    vmem = pl.BlockSpec(memory_space=pltpu.VMEM)

    def settings(mebibytes, microseconds):
        return dict(
            compiler_params=pltpu.CompilerParams(
                vmem_limit_bytes=mebibytes << 20
            ),
            cost_estimate=pl.CostEstimate(
                flops=int(microseconds * 1.1e9), bytes_accessed=8 << 20, transcendentals=0
            ),
        )


    levels = devices.bit_length() - 1
    place = lax.axis_index("enc")
    bits = [(place >> level) & 1 for level in range(levels)]
    firsts, core, work = lax.optimization_barrier(
        ([bit == 0 for bit in bits], bits[0].reshape(1, 1), jnp.transpose(tiles, (1, 0, 2)))
    )
    before, sums = pl.pallas_call(
        functools.partial(conv_kernel, cap_rows),
        in_specs=[vmem] * 3,
        out_specs=[vmem] * 2,
        out_shape=[
            jax.ShapeDtypeStruct((positions, own_rows, emb_width), f32),
            jax.ShapeDtypeStruct((2, devices, emb_width), f32),
        ],
        name="conv_sums",
        **settings(20, 6),
    )(work, assign, w_conv)
    total = SmallSum(sums, firsts)
    for level in range(1, levels):
        total.hop(level)
    first, second = total.result()

    half_rows = (emb_width + hid_width) // 2
    send, keep, grad_embedded, sums = pl.pallas_call(
        functools.partial(head_kernel, cap_rows, pixel_count, slides_all),
        in_specs=[smem] * 3 + [vmem] * 10,
        out_specs=[vmem] * 4,
        out_shape=[
            jax.ShapeDtypeStruct((half_rows, hid_width), bf16),
            jax.ShapeDtypeStruct((half_rows, hid_width), f32),
            jax.ShapeDtypeStruct((own_rows, emb_width), bf16),
            jax.ShapeDtypeStruct((2, devices, emb_width + EXTRA), f32),
        ],
        scratch_shapes=[
            pltpu.VMEM((own_rows, emb_width), bf16),
            pltpu.VMEM((own_rows, emb_width), f32),
            pltpu.VMEM((own_rows, emb_width), f32),
            pltpu.VMEM((2, half_rows, hid_width), f32),
        ],
        name="norm_head",
        **settings(32, 12),
    )(
        tile_counts,
        labels,
        core,
        before,
        assign,
        first,
        second,
        gain,
        shift,
        w_fc,
        w_gate,
        w_score.reshape(1, -1),
        w_cls.T,
    )
    total = SmallSum(sums, firsts)
    rows_fc = emb_width // 2
    head = LargeSum(keep + swap(send, 0).astype(f32), firsts)
    total.hop(1)
    total.x = wait_for(total.x, head.x)
    head.halve(1)
    for level in range(2, levels):
        total.hop(level)
    total.x = wait_for(total.x, head.x)
    shift_sums, gain_sums = total.result()

    grad_conv, grad_gain, grad_shift = pl.pallas_call(
        functools.partial(back_kernel, cap_rows, pixel_count),
        in_specs=[vmem] * 10,
        out_specs=[vmem] * 3,
        out_shape=[
            jax.ShapeDtypeStruct((input_width, emb_width), f32),
            jax.ShapeDtypeStruct((1, emb_width), f32),
            jax.ShapeDtypeStruct((1, emb_width), f32),
        ],
        name="norm_back",
        **settings(20, 7),
    )(work, before, grad_embedded, assign, first, second, shift_sums, gain_sums, gain, shift)

    conv = LargeSum(grad_conv, firsts)
    for level in range(2, levels - 1):
        head.halve(level)
    conv.halve(0, head.x)
    conv.halve(1)
    head.exchange(levels - 1)
    head.x = wait_for(head.x, conv.x)
    for level in range(2, levels - 1):
        conv.halve(level)
    for level in range(levels - 2, 1, -1):
        head.double(level)
    head.x = wait_for(head.x, conv.x)
    conv.exchange(levels - 1)
    conv.x = wait_for(conv.x, head.x)
    for level in range(levels - 2, 1, -1):
        conv.double(level)
    head.double(1)
    conv.x = wait_for(conv.x, head.x)
    conv.double(1)
    low, high = head.pair(0)
    grad_fc = jnp.concatenate([low[:rows_fc], high[:rows_fc]], axis=0).astype(f32)
    grad_gate = jnp.concatenate([low[rows_fc:], high[rows_fc:]], axis=0).astype(f32)
    conv.x = wait_for(conv.x, grad_fc)
    conv.double(0)
    grad_conv = conv.x.astype(f32)
    scores = w_score.shape[0] // EXTRA
    classes = math.prod(w_cls.shape) // EXTRA
    return (
        shift_sums[scores, emb_width : emb_width + 1],
        grad_conv,
        grad_gain.reshape(emb_width),
        grad_shift.reshape(emb_width),
        grad_fc,
        grad_gate,
        shift_sums[:scores, emb_width:].reshape(-1),
        gain_sums[:classes, emb_width:].reshape(w_cls.shape[::-1]).T,
    )


def solution(mesh):
    per_device = P(("groups", "enc"), None)
    placed = (P(("groups", "enc"), None, None), per_device, per_device, per_device) + (P(),) * 7
    rows_out = P("groups", None)
    return jax.shard_map(
        local,
        mesh=mesh,
        in_specs=placed,
        out_specs=(
            P("groups"),
            rows_out,
            P("groups"),
            P("groups"),
            rows_out,
            rows_out,
            P("groups"),
            rows_out,
        ),
        check_vma=False,
    )
```

```python
import functools

import jax
import jax.numpy as jnp
from jax import lax
from jax.experimental import pallas as pl
from jax.experimental.pallas import tpu as pltpu
from jax.sharding import PartitionSpec as P

epsilon = 1e-05
f32, bf16 = jnp.float32, jnp.bfloat16
CHUNK_CONV, CHUNK_HEAD, CHUNK_BACK = 128, 128, 128
EXTRA = 128


def split3(x):
    high = x.astype(bf16)
    rest = x - high.astype(f32)
    middle = rest.astype(bf16)
    low = (rest - middle.astype(f32)).astype(bf16)
    return high, middle, low


def contract_rows(left, right):
    return lax.dot_general(
        left, right, (((0,), (0,)), ((), ())), preferred_element_type=f32
    )


def contract_cols(left, right):
    return lax.dot_general(
        left, right, (((1,), (1,)), ((), ())), preferred_element_type=f32
    )


def matmul(left, right):
    return jnp.dot(left, right, preferred_element_type=f32)


def one_hot(assign, groups, cap_rows):
    low = lax.broadcasted_iota(jnp.int32, (groups, assign.shape[1]), 0) * cap_rows
    return jnp.where((assign >= low) & (assign < low + cap_rows), 1.0, 0.0)


def group_sums(member, values):
    high = values.astype(bf16)
    low = (values - high.astype(f32)).astype(bf16)
    return matmul(member, high) + matmul(member, low)


def spread(member, values):
    return contract_rows(
        jnp.concatenate([member] * 3, axis=0).astype(bf16),
        jnp.concatenate(split3(values), axis=0),
    )


def moments(first, second, pixel_count):
    mean = first * (1.0 / pixel_count)
    variance = second * (1.0 / pixel_count) - mean * mean
    return mean, lax.rsqrt(variance + epsilon)


def conv_kernel(cap_rows, x_ref, assign_ref, w_ref, before_ref, sums_ref):
    positions, tiles_all, width = x_ref.shape
    groups, emb_width = sums_ref.shape[1:]
    tiles = CHUNK_CONV
    inputs = jnp.zeros((groups, width), f32)
    squares = jnp.zeros((groups, emb_width), f32)
    for start in range(0, tiles_all, tiles):
        rows = pl.ds(start, tiles)
        x = x_ref[:, rows].reshape(positions * tiles, width)
        before = matmul(x, w_ref[...])
        before_ref[:, rows] = before.reshape(positions, tiles, emb_width)
        parts = [before[p * tiles : (p + 1) * tiles] for p in range(positions)]
        second = sum([v * v for v in parts[1:]], parts[0] * parts[0])
        member = one_hot(assign_ref[:, rows], groups, cap_rows).astype(bf16)
        inputs += matmul(jnp.concatenate([member] * positions, axis=1), x)
        squares += group_sums(member, second)
    terms = matmul(jnp.concatenate(split3(inputs), axis=0), w_ref[...])
    sums_ref[0] = terms[:groups] + terms[groups : 2 * groups] + terms[2 * groups :]
    sums_ref[1] = squares


def head_kernel(
    cap_rows,
    pixel_count,
    slides_all,
    counts_ref,
    labels_ref,
    core_ref,
    before_ref,
    assign_ref,
    first_ref,
    second_ref,
    gain_ref,
    shift_ref,
    w_fc_ref,
    w_gate_ref,
    w_score_ref,
    w_cls_ref,
    send_ref,
    keep_ref,
    grad_embedded_ref,
    sums_ref,
    embedded_ref,
    count_ref,
    total_ref,
    grad_ref,
):
    positions, tiles_all, emb_width = before_ref.shape
    tiles = CHUNK_HEAD
    groups = first_ref.shape[0]
    mean, inverse = moments(first_ref[...], second_ref[...], pixel_count)
    scale = inverse * gain_ref[...]
    offset = shift_ref[...] - mean * scale
    both = jnp.concatenate([scale, offset], axis=1)
    for begin in range(0, tiles_all, tiles):
        rows = pl.ds(begin, tiles)
        spread_rows = spread(one_hot(assign_ref[:, rows], groups, cap_rows), both)
        scale, offset = spread_rows[:, :emb_width], spread_rows[:, emb_width:]
        count = jnp.zeros((tiles, emb_width), f32)
        total = jnp.zeros((tiles, emb_width), f32)
        for p in range(positions):
            value = before_ref[p, rows]
            live = value * scale + offset > 0
            count += jnp.where(live, 1.0, 0.0)
            total += jnp.where(live, value, 0.0)
        embedded_ref[rows] = ((total * scale + count * offset) * (1.0 / positions)).astype(bf16)
        count_ref[rows] = count
        total_ref[rows] = total

    embedded = embedded_ref[...]
    slides = counts_ref.shape[1]
    pre = matmul(embedded, w_fc_ref[...])
    hidden = jnp.maximum(pre, 0.0).astype(bf16)
    gate_pre = matmul(hidden, w_gate_ref[...])
    half = gate_pre.shape[1] // 2
    wave = jnp.tanh(gate_pre[:, :half])
    sig = jax.nn.sigmoid(gate_pre[:, half:])
    mix = wave * sig
    w_score = w_score_ref[...]
    score = jnp.sum(mix * w_score, axis=1, keepdims=True)

    lane = lax.broadcasted_iota(jnp.int32, (1, 128), 1)
    row = lax.broadcasted_iota(jnp.int32, (tiles_all, 128), 0)
    low = jnp.zeros((1, 128), jnp.int32)
    high = jnp.zeros((1, 128), jnp.int32)
    start = jnp.int32(0)
    for s in range(slides):
        end = start + counts_ref[0, s]
        low = jnp.where(lane == s, start, low)
        high = jnp.where(lane == s, end, high)
        start = end
    weight = jnp.where((row >= low) & (row < high), jnp.exp(score), 0.0)
    totals = jnp.sum(weight, axis=0, keepdims=True)
    attention = weight / jnp.where(lane < slides, totals, 1.0)
    att_high, att_middle, att_low = split3(attention)
    pooled = (
        contract_rows(att_high, hidden)
        + contract_rows(att_middle, hidden)
        + contract_rows(att_low, hidden)
    )[:8]
    slot = lax.broadcasted_iota(jnp.int32, (8, 1), 0)
    label = jnp.zeros((8, 1), jnp.int32)
    for s in range(slides):
        label = jnp.where(slot == s, labels_ref[0, s], label)
    classes = w_cls_ref.shape[0]
    w_cls = [w_cls_ref[c : c + 1, :] for c in range(classes)]
    logits = [jnp.sum(pooled * w, axis=1, keepdims=True) for w in w_cls]
    powers = [jnp.exp(v) for v in logits]
    power = sum(powers[1:], powers[0])
    target = sum(jnp.where(label == c, v, 0.0) for c, v in enumerate(logits))
    used = slot < slides
    loss = jnp.sum(jnp.where(used, jnp.log(power) - target, 0.0), axis=0, keepdims=True) * (
        1.0 / slides_all
    )
    grad_logits = [
        jnp.where(used, v / power - jnp.where(label == c, 1.0, 0.0), 0.0) * (1.0 / slides_all)
        for c, v in enumerate(powers)
    ]
    grad_cls = [jnp.sum(g * pooled, axis=0, keepdims=True) for g in grad_logits]
    grad_pooled = sum(g * w for g, w in zip(grad_logits, w_cls))
    grad_pooled = jnp.concatenate(
        [grad_pooled, jnp.zeros((128 - 8, grad_pooled.shape[1]), f32)], axis=0
    )
    gp_high, gp_middle, gp_low = split3(grad_pooled)
    grad_attention = (
        contract_cols(hidden, gp_high)
        + contract_cols(hidden, gp_middle)
        + contract_cols(hidden, gp_low)
    )
    product = attention * grad_attention
    centre = jnp.sum(product, axis=0, keepdims=True)
    grad_score = jnp.sum(product - attention * centre, axis=1, keepdims=True)
    grad_w_score = jnp.sum(grad_score * mix, axis=0, keepdims=True)
    grad_mix = grad_score * w_score
    gates_low = jnp.concatenate(
        [grad_mix * sig * (1.0 - wave * wave), grad_mix * mix * (1.0 - sig)], axis=1
    ).astype(bf16)
    grad_hidden = matmul(
        jnp.concatenate([att_high, att_high, att_middle], axis=1),
        jnp.concatenate([gp_high, gp_middle, gp_high], axis=0),
    )
    grad_hidden += contract_cols(gates_low, w_gate_ref[...])
    before_low = jnp.where(pre > 0, grad_hidden, 0.0).astype(bf16)
    core = core_ref[0, 0]
    rows_fc, rows_gate = emb_width // 2, pre.shape[1] // 2
    halves_fc = grad_ref.at[:, pl.ds(0, rows_fc)]
    halves_gate = grad_ref.at[:, pl.ds(rows_fc, rows_gate)]
    halves_fc[...] = contract_rows(embedded, before_low).reshape(2, rows_fc, -1)
    halves_gate[...] = contract_rows(hidden, gates_low).reshape(2, rows_gate, -1)
    send_ref[...] = grad_ref[1 - core].astype(bf16)
    keep_ref[...] = grad_ref[core]
    grad_embedded = contract_cols(before_low, w_fc_ref[...]).astype(bf16)
    grad_embedded_ref[...] = grad_embedded
    each = grad_embedded.astype(f32) * (1.0 / positions)
    member_all = one_hot(assign_ref[...], groups, cap_rows).astype(bf16)
    shift_sums = group_sums(member_all, each * count_ref[...])
    total_sums = group_sums(member_all, each * total_ref[...])
    sums_ref[0, :, :emb_width] = shift_sums
    sums_ref[1, :, :emb_width] = (total_sums - mean * shift_sums) * inverse
    sums_ref[:, :, emb_width:] = jnp.zeros((2, groups, EXTRA), f32)
    for i in range(half // EXTRA):
        sums_ref[0, i : i + 1, emb_width:] = grad_w_score[:, i * EXTRA : (i + 1) * EXTRA]
    i = half // EXTRA
    sums_ref[0, i : i + 1, emb_width:] = jnp.where(lane == 0, loss, 0.0)
    grad_cls = jnp.concatenate(grad_cls, axis=1)
    for i in range(grad_cls.shape[1] // EXTRA):
        sums_ref[1, i : i + 1, emb_width:] = grad_cls[:, i * EXTRA : (i + 1) * EXTRA]


def back_kernel(
    cap_rows,
    pixel_count,
    x_ref,
    before_ref,
    grad_embedded_ref,
    assign_ref,
    first_ref,
    second_ref,
    shift_sums_ref,
    gain_sums_ref,
    gain_ref,
    shift_ref,
    grad_ref,
    grad_gain_ref,
    grad_shift_ref,
    grad_score_ref,
    grad_cls_ref,
    loss_ref,
):

    positions, tiles_all, emb_width = before_ref.shape
    tiles = CHUNK_BACK
    groups = first_ref.shape[0]
    mean, inverse = moments(first_ref[...], second_ref[...], pixel_count)
    scale = inverse * gain_ref[...]
    offset = shift_ref[...] - mean * scale
    slope = scale * inverse * gain_sums_ref[:, :emb_width] * (1.0 / pixel_count)
    constant = scale * shift_sums_ref[:, :emb_width] * (1.0 / pixel_count) - mean * slope
    grad_gain_ref[...] = jnp.sum(gain_sums_ref[:, :emb_width], axis=0, keepdims=True)
    grad_shift_ref[...] = jnp.sum(shift_sums_ref[:, :emb_width], axis=0, keepdims=True)
    scores = grad_score_ref.shape[1] // EXTRA
    for i in range(scores):
        grad_score_ref[:, i * EXTRA : (i + 1) * EXTRA] = shift_sums_ref[i : i + 1, emb_width:]
    loss_ref[...] = shift_sums_ref[scores : scores + 1, emb_width : emb_width + 1]
    classes, hid_width = grad_cls_ref.shape
    for c in range(classes):
        for i in range(hid_width // EXTRA):
            spot = c * (hid_width // EXTRA) + i
            grad_cls_ref[c : c + 1, i * EXTRA : (i + 1) * EXTRA] = gain_sums_ref[
                spot : spot + 1, emb_width:
            ]
    every = jnp.concatenate([scale, offset, slope, constant], axis=1)
    for start in range(0, tiles_all, tiles):
        rows = pl.ds(start, tiles)
        spread_rows = spread(one_hot(assign_ref[:, rows], groups, cap_rows), every)
        scale, offset, slope, constant = (
            spread_rows[:, i * emb_width : (i + 1) * emb_width] for i in range(4)
        )
        direct = grad_embedded_ref[rows].astype(f32) * scale * (1.0 / positions)
        grads = []
        for p in range(positions):
            value = before_ref[p, rows]
            live = value * scale + offset > 0
            grads.append((jnp.where(live, direct, 0.0) - constant - value * slope).astype(bf16))
        part = contract_rows(
            x_ref[:, rows].reshape(positions * tiles, x_ref.shape[2]),
            jnp.concatenate(grads, axis=0),
        )
        if start == 0:
            grad_ref[...] = part
        else:
            grad_ref[...] += part


def finish_kernel(
    core_ref,
    head_ref,
    head_other_ref,
    conv_ref,
    conv_other_ref,
    fc_out,
    gate_out,
    conv_out,
    fc_ref,
    gate_ref,
    conv_wide_ref,
    copied,
):
    core = core_ref[0, 0]
    copies = []

    def place(value, spot, wide_ref, out):
        half = value.shape[0]
        rows = pl.ds(pl.multiple_of(spot * half, half), half)
        wide_ref[rows] = value.astype(f32)
        copies.append(
            pltpu.make_async_copy(wide_ref.at[rows], out.at[rows], copied.at[len(copies)])
        )
        copies[-1].start()

    rows_fc = fc_ref.shape[0] // 2
    for ref, spot in ((head_ref, core), (head_other_ref, 1 - core)):
        place(ref[:rows_fc], spot, fc_ref, fc_out)
        place(ref[rows_fc:], spot, gate_ref, gate_out)
    for ref, spot in ((conv_ref, core), (conv_other_ref, 1 - core)):
        place(ref[...], spot, conv_wide_ref, conv_out)
    for c in copies:
        c.wait()


def round_low(x):
    return lax.reduce_precision(x, 8, 7)


def swap(x, *levels):
    mask = sum(1 << level for level in levels)
    count = lax.axis_size("enc")
    return lax.ppermute(x, "enc", [(i, i ^ mask) for i in range(count)])


def wait_for(x, other):
    rows = min(16, x.shape[0], other.shape[0])
    corner = (other[:rows, :128] * 0).astype(x.dtype)
    return x + jnp.pad(corner, ((0, x.shape[0] - rows), (0, x.shape[1] - 128)))


class SmallSum:
    def __init__(self, pair, firsts):
        self.core = firsts[0]
        self.x = jnp.where(self.core, pair[0], pair[1])
        self.x += swap(jnp.where(self.core, pair[1], pair[0]), 0)

    def hop(self, level):
        self.x += swap(self.x, level)

    def cross(self, one, two):
        x = self.x
        self.x = (x + swap(x, one)) + (swap(x, two) + swap(x, one, two))

    def result(self):
        other = swap(self.x, 0)
        return jnp.where(self.core, self.x, other), jnp.where(self.core, other, self.x)


class LargeSum:
    def __init__(self, x, firsts):
        self.x = x
        self.firsts = firsts

    def halve(self, level, other=None):
        half = self.x.shape[0] // 2
        low, high = self.x[:half], self.x[half:]
        first = self.firsts[level]
        send = jnp.where(first, high, low).astype(bf16)
        if other is not None:
            send = wait_for(send, other)
        self.x = jnp.where(first, low, high) + swap(send, level).astype(f32)

    def exchange(self, level):
        x = round_low(self.x)
        self.x = (x + swap(x.astype(bf16), level).astype(f32)).astype(bf16)

    def pair(self, level):
        other = swap(self.x, level)
        first = self.firsts[level]
        return jnp.where(first, self.x, other), jnp.where(first, other, self.x)

    def double(self, level):
        self.x = jnp.concatenate(self.pair(level), axis=0)


def local(
    tiles, tile_counts, assign, labels, w_conv, bn_gain, bn_shift, w_fc, w_gate, w_score, w_cls
):
    devices = lax.axis_size("enc")
    own_rows, positions, input_width = tiles.shape
    emb_width = w_conv.shape[1]
    hid_width = w_fc.shape[1]
    slot_rows = assign.shape[1]
    cap_rows = slot_rows // devices
    group_tiles = (
        devices // 4 * (4 + (cap_rows - 2) // 3 + 2 * (cap_rows - 2) // 3 + (cap_rows - 2))
        + devices // 2
    )
    pixel_count = float(group_tiles * positions)
    slides_all = float(devices * tile_counts.shape[1])
    gain, shift = bn_gain.reshape(1, emb_width), bn_shift.reshape(1, emb_width)

    smem = pl.BlockSpec(memory_space=pltpu.SMEM)
    vmem = pl.BlockSpec(memory_space=pltpu.VMEM)

    def settings(mebibytes, microseconds):
        return dict(
            compiler_params=pltpu.CompilerParams(
                vmem_limit_bytes=mebibytes << 20
            ),
            cost_estimate=pl.CostEstimate(
                flops=int(microseconds * 1.1e9), bytes_accessed=8 << 20, transcendentals=0
            ),
        )


    levels = devices.bit_length() - 1
    place = lax.axis_index("enc")
    bits = [(place >> level) & 1 for level in range(levels)]
    firsts, core, work = lax.optimization_barrier(
        ([bit == 0 for bit in bits], bits[0].reshape(1, 1), jnp.transpose(tiles, (1, 0, 2)))
    )
    before, sums = pl.pallas_call(
        functools.partial(conv_kernel, cap_rows),
        in_specs=[vmem] * 3,
        out_specs=[vmem] * 2,
        out_shape=[
            jax.ShapeDtypeStruct((positions, own_rows, emb_width), f32),
            jax.ShapeDtypeStruct((2, devices, emb_width), f32),
        ],
        name="conv_sums",
        **settings(20, 6),
    )(work, assign, w_conv)
    total = SmallSum(sums, firsts)
    total.cross(1, 2)
    for level in range(3, levels):
        total.hop(level)
    first, second = total.result()

    half_rows = (emb_width + hid_width) // 2
    send, keep, grad_embedded, sums = pl.pallas_call(
        functools.partial(head_kernel, cap_rows, pixel_count, slides_all),
        in_specs=[smem] * 3 + [vmem] * 10,
        out_specs=[vmem] * 4,
        out_shape=[
            jax.ShapeDtypeStruct((half_rows, hid_width), bf16),
            jax.ShapeDtypeStruct((half_rows, hid_width), f32),
            jax.ShapeDtypeStruct((own_rows, emb_width), bf16),
            jax.ShapeDtypeStruct((2, devices, emb_width + EXTRA), f32),
        ],
        scratch_shapes=[
            pltpu.VMEM((own_rows, emb_width), bf16),
            pltpu.VMEM((own_rows, emb_width), f32),
            pltpu.VMEM((own_rows, emb_width), f32),
            pltpu.VMEM((2, half_rows, hid_width), f32),
        ],
        name="norm_head",
        **settings(32, 12),
    )(
        tile_counts,
        labels,
        core,
        before,
        assign,
        first,
        second,
        gain,
        shift,
        w_fc,
        w_gate,
        w_score.reshape(1, -1),
        w_cls.T,
    )
    total = SmallSum(sums, firsts)
    head = LargeSum(keep + swap(send, 0).astype(f32), firsts)
    total.cross(1, 2)
    total.x = wait_for(total.x, head.x)
    head.halve(1)
    for level in range(3, levels):
        total.hop(level)
    total.x = wait_for(total.x, head.x)
    shift_sums, gain_sums = total.result()

    grad_conv, grad_gain, grad_shift, grad_score, grad_cls, loss = pl.pallas_call(
        functools.partial(back_kernel, cap_rows, pixel_count),
        in_specs=[vmem] * 10,
        out_specs=[vmem] * 6,
        out_shape=[
            jax.ShapeDtypeStruct((input_width, emb_width), f32),
            jax.ShapeDtypeStruct((1, emb_width), f32),
            jax.ShapeDtypeStruct((1, emb_width), f32),
            jax.ShapeDtypeStruct((1, w_score.shape[0]), f32),
            jax.ShapeDtypeStruct(w_cls.shape[::-1], f32),
            jax.ShapeDtypeStruct((1, 1), f32),
        ],
        name="norm_back",
        **settings(20, 7),
    )(work, before, grad_embedded, assign, first, second, shift_sums, gain_sums, gain, shift)

    conv = LargeSum(grad_conv, firsts)
    for level in range(2, levels - 1):
        head.halve(level)
    conv.halve(0, head.x)
    conv.halve(1)
    head.exchange(levels - 1)
    head.x = wait_for(head.x, conv.x)
    for level in range(2, levels - 1):
        conv.halve(level)
    for level in range(levels - 2, 1, -1):
        head.double(level)
    head.x = wait_for(head.x, conv.x)
    conv.exchange(levels - 1)
    conv.x = wait_for(conv.x, head.x)
    for level in range(levels - 2, 1, -1):
        conv.double(level)
    head.double(1)
    conv.x = wait_for(conv.x, head.x)
    conv.double(1)
    head_other = swap(head.x, 0)
    conv.x = wait_for(conv.x, head_other)
    wide = [(emb_width, hid_width), (hid_width, hid_width), (input_width, emb_width)]
    grad_fc, grad_gate, grad_conv = pl.pallas_call(
        finish_kernel,
        in_specs=[smem] + [vmem] * 4,
        out_specs=[pl.BlockSpec(memory_space=pl.ANY)] * 3,
        out_shape=[jax.ShapeDtypeStruct(shape, f32) for shape in wide],
        scratch_shapes=[pltpu.VMEM(shape, f32) for shape in wide]
        + [pltpu.SemaphoreType.DMA((6,))],
        name="finish",
        **settings(12, 3),
    )(core, head.x, head_other, conv.x, swap(conv.x, 0))
    return (
        loss.reshape(1),
        grad_conv,
        grad_gain.reshape(emb_width),
        grad_shift.reshape(emb_width),
        grad_fc,
        grad_gate,
        grad_score.reshape(-1),
        grad_cls.T,
    )


def solution(mesh):
    per_device = P(("groups", "enc"), None)
    placed = (P(("groups", "enc"), None, None), per_device, per_device, per_device) + (P(),) * 7
    rows_out = P("groups", None)
    return jax.shard_map(
        local,
        mesh=mesh,
        in_specs=placed,
        out_specs=(
            P("groups"),
            rows_out,
            P("groups"),
            P("groups"),
            rows_out,
            rows_out,
            P("groups"),
            rows_out,
        ),
        check_vma=False,
    )
```

```python
import functools

import jax
import jax.numpy as jnp
from jax import lax
from jax.experimental import pallas as pl
from jax.experimental.pallas import tpu as pltpu
from jax.sharding import PartitionSpec as P

epsilon = 1e-05
f32, bf16 = jnp.float32, jnp.bfloat16
CHUNK_CONV, CHUNK_HEAD, CHUNK_BACK = 256, 256, 128
EXTRA = 128


def split3(x):
    high = x.astype(bf16)
    rest = x - high.astype(f32)
    middle = rest.astype(bf16)
    low = (rest - middle.astype(f32)).astype(bf16)
    return high, middle, low


def contract_rows(left, right):
    return lax.dot_general(
        left, right, (((0,), (0,)), ((), ())), preferred_element_type=f32
    )


def contract_cols(left, right):
    return lax.dot_general(
        left, right, (((1,), (1,)), ((), ())), preferred_element_type=f32
    )


def matmul(left, right):
    return jnp.dot(left, right, preferred_element_type=f32)


def one_hot(assign, groups, cap_rows):
    low = lax.broadcasted_iota(jnp.int32, (groups, assign.shape[1]), 0) * cap_rows
    return jnp.where((assign >= low) & (assign < low + cap_rows), 1.0, 0.0)


def group_sums(member, values):
    high = values.astype(bf16)
    low = (values - high.astype(f32)).astype(bf16)
    return matmul(member, high) + matmul(member, low)


def spread(member, values):
    return contract_rows(
        jnp.concatenate([member] * 3, axis=0).astype(bf16),
        jnp.concatenate(split3(values), axis=0),
    )


def moments(first, second, pixel_count):
    mean = first * (1.0 / pixel_count)
    variance = second * (1.0 / pixel_count) - mean * mean
    return mean, lax.rsqrt(variance + epsilon)


def conv_kernel(cap_rows, x_ref, assign_ref, w_ref, before_ref, sums_ref):
    positions, tiles_all, width = x_ref.shape
    groups, emb_width = sums_ref.shape[1:]
    tiles = CHUNK_CONV
    inputs = jnp.zeros((groups, width), f32)
    squares = jnp.zeros((groups, emb_width), f32)
    for start in range(0, tiles_all, tiles):
        rows = pl.ds(start, tiles)
        x = x_ref[:, rows].reshape(positions * tiles, width)
        before = matmul(x, w_ref[...])
        before_ref[:, rows] = before.reshape(positions, tiles, emb_width)
        parts = [before[p * tiles : (p + 1) * tiles] for p in range(positions)]
        second = sum([v * v for v in parts[1:]], parts[0] * parts[0])
        member = one_hot(assign_ref[:, rows], groups, cap_rows).astype(bf16)
        inputs += matmul(jnp.concatenate([member] * positions, axis=1), x)
        squares += group_sums(member, second)
    terms = matmul(jnp.concatenate(split3(inputs), axis=0), w_ref[...])
    sums_ref[0] = terms[:groups] + terms[groups : 2 * groups] + terms[2 * groups :]
    sums_ref[1] = squares


def head_kernel(
    cap_rows,
    pixel_count,
    slides_all,
    counts_ref,
    labels_ref,
    core_ref,
    before_ref,
    assign_ref,
    first_ref,
    second_ref,
    gain_ref,
    shift_ref,
    w_fc_ref,
    w_gate_ref,
    w_score_ref,
    w_cls_ref,
    send_ref,
    keep_ref,
    grad_embedded_ref,
    sums_ref,
    embedded_ref,
    count_ref,
    total_ref,
    grad_ref,
):
    positions, tiles_all, emb_width = before_ref.shape
    tiles = CHUNK_HEAD
    groups = first_ref.shape[0]
    mean, inverse = moments(first_ref[...], second_ref[...], pixel_count)
    scale = inverse * gain_ref[...]
    offset = shift_ref[...] - mean * scale
    both = jnp.concatenate([scale, offset], axis=1)
    for begin in range(0, tiles_all, tiles):
        rows = pl.ds(begin, tiles)
        spread_rows = spread(one_hot(assign_ref[:, rows], groups, cap_rows), both)
        scale, offset = spread_rows[:, :emb_width], spread_rows[:, emb_width:]
        count = jnp.zeros((tiles, emb_width), f32)
        total = jnp.zeros((tiles, emb_width), f32)
        for p in range(positions):
            value = before_ref[p, rows]
            live = value * scale + offset > 0
            count += jnp.where(live, 1.0, 0.0)
            total += jnp.where(live, value, 0.0)
        embedded_ref[rows] = ((total * scale + count * offset) * (1.0 / positions)).astype(bf16)
        count_ref[rows] = count
        total_ref[rows] = total

    embedded = embedded_ref[...]
    slides = counts_ref.shape[1]
    pre = matmul(embedded, w_fc_ref[...])
    hidden = jnp.maximum(pre, 0.0).astype(bf16)
    gate_pre = matmul(hidden, w_gate_ref[...])
    half = gate_pre.shape[1] // 2
    wave = jnp.tanh(gate_pre[:, :half])
    sig = jax.nn.sigmoid(gate_pre[:, half:])
    mix = wave * sig
    w_score = w_score_ref[...]
    score = jnp.sum(mix * w_score, axis=1, keepdims=True)

    lane = lax.broadcasted_iota(jnp.int32, (1, 128), 1)
    row = lax.broadcasted_iota(jnp.int32, (tiles_all, 128), 0)
    low = jnp.zeros((1, 128), jnp.int32)
    high = jnp.zeros((1, 128), jnp.int32)
    start = jnp.int32(0)
    for s in range(slides):
        end = start + counts_ref[0, s]
        low = jnp.where(lane == s, start, low)
        high = jnp.where(lane == s, end, high)
        start = end
    weight = jnp.where((row >= low) & (row < high), jnp.exp(score), 0.0)
    totals = jnp.sum(weight, axis=0, keepdims=True)
    attention = weight / jnp.where(lane < slides, totals, 1.0)
    att_high, att_middle, att_low = split3(attention)
    pooled = (
        contract_rows(att_high, hidden)
        + contract_rows(att_middle, hidden)
        + contract_rows(att_low, hidden)
    )[:8]
    slot = lax.broadcasted_iota(jnp.int32, (8, 1), 0)
    label = jnp.zeros((8, 1), jnp.int32)
    for s in range(slides):
        label = jnp.where(slot == s, labels_ref[0, s], label)
    classes = w_cls_ref.shape[0]
    w_cls = [w_cls_ref[c : c + 1, :] for c in range(classes)]
    logits = [jnp.sum(pooled * w, axis=1, keepdims=True) for w in w_cls]
    powers = [jnp.exp(v) for v in logits]
    power = sum(powers[1:], powers[0])
    target = sum(jnp.where(label == c, v, 0.0) for c, v in enumerate(logits))
    used = slot < slides
    loss = jnp.sum(jnp.where(used, jnp.log(power) - target, 0.0), axis=0, keepdims=True) * (
        1.0 / slides_all
    )
    grad_logits = [
        jnp.where(used, v / power - jnp.where(label == c, 1.0, 0.0), 0.0) * (1.0 / slides_all)
        for c, v in enumerate(powers)
    ]
    grad_cls = [jnp.sum(g * pooled, axis=0, keepdims=True) for g in grad_logits]
    grad_pooled = sum(g * w for g, w in zip(grad_logits, w_cls))
    grad_pooled = jnp.concatenate(
        [grad_pooled, jnp.zeros((128 - 8, grad_pooled.shape[1]), f32)], axis=0
    )
    gp_high, gp_middle, gp_low = split3(grad_pooled)
    grad_attention = (
        contract_cols(hidden, gp_high)
        + contract_cols(hidden, gp_middle)
        + contract_cols(hidden, gp_low)
    )
    product = attention * grad_attention
    centre = jnp.sum(product, axis=0, keepdims=True)
    grad_score = jnp.sum(product - attention * centre, axis=1, keepdims=True)
    grad_w_score = jnp.sum(grad_score * mix, axis=0, keepdims=True)
    grad_mix = grad_score * w_score
    gates_low = jnp.concatenate(
        [grad_mix * sig * (1.0 - wave * wave), grad_mix * mix * (1.0 - sig)], axis=1
    ).astype(bf16)
    grad_hidden = matmul(
        jnp.concatenate([att_high, att_high, att_middle], axis=1),
        jnp.concatenate([gp_high, gp_middle, gp_high], axis=0),
    )
    grad_hidden += contract_cols(gates_low, w_gate_ref[...])
    before_low = jnp.where(pre > 0, grad_hidden, 0.0).astype(bf16)
    core = core_ref[0, 0]
    rows_fc, rows_gate = emb_width // 2, pre.shape[1] // 2
    halves_fc = grad_ref.at[:, pl.ds(0, rows_fc)]
    halves_gate = grad_ref.at[:, pl.ds(rows_fc, rows_gate)]
    halves_fc[...] = contract_rows(embedded, before_low).reshape(2, rows_fc, -1)
    halves_gate[...] = contract_rows(hidden, gates_low).reshape(2, rows_gate, -1)
    send_ref[...] = grad_ref[1 - core].astype(bf16)
    keep_ref[...] = grad_ref[core]
    grad_embedded = contract_cols(before_low, w_fc_ref[...]).astype(bf16)
    grad_embedded_ref[...] = grad_embedded
    each = grad_embedded.astype(f32) * (1.0 / positions)
    member_all = one_hot(assign_ref[...], groups, cap_rows).astype(bf16)
    shift_sums = group_sums(member_all, each * count_ref[...])
    total_sums = group_sums(member_all, each * total_ref[...])
    sums_ref[0, :, :emb_width] = shift_sums
    sums_ref[1, :, :emb_width] = (total_sums - mean * shift_sums) * inverse
    sums_ref[:, :, emb_width:] = jnp.zeros((2, groups, EXTRA), f32)
    for i in range(half // EXTRA):
        sums_ref[0, i : i + 1, emb_width:] = grad_w_score[:, i * EXTRA : (i + 1) * EXTRA]
    i = half // EXTRA
    sums_ref[0, i : i + 1, emb_width:] = jnp.where(lane == 0, loss, 0.0)
    grad_cls = jnp.concatenate(grad_cls, axis=1)
    for i in range(grad_cls.shape[1] // EXTRA):
        sums_ref[1, i : i + 1, emb_width:] = grad_cls[:, i * EXTRA : (i + 1) * EXTRA]


def back_kernel(
    cap_rows,
    pixel_count,
    x_ref,
    before_ref,
    grad_embedded_ref,
    assign_ref,
    first_ref,
    second_ref,
    shift_sums_ref,
    gain_sums_ref,
    gain_ref,
    shift_ref,
    grad_ref,
    grad_gain_ref,
    grad_shift_ref,
    grad_score_ref,
    grad_cls_ref,
    loss_ref,
):

    positions, tiles_all, emb_width = before_ref.shape
    tiles = CHUNK_BACK
    groups = first_ref.shape[0]
    mean, inverse = moments(first_ref[...], second_ref[...], pixel_count)
    scale = inverse * gain_ref[...]
    offset = shift_ref[...] - mean * scale
    slope = scale * inverse * gain_sums_ref[:, :emb_width] * (1.0 / pixel_count)
    constant = scale * shift_sums_ref[:, :emb_width] * (1.0 / pixel_count) - mean * slope
    grad_gain_ref[...] = jnp.sum(gain_sums_ref[:, :emb_width], axis=0, keepdims=True)
    grad_shift_ref[...] = jnp.sum(shift_sums_ref[:, :emb_width], axis=0, keepdims=True)
    scores = grad_score_ref.shape[1] // EXTRA
    for i in range(scores):
        grad_score_ref[:, i * EXTRA : (i + 1) * EXTRA] = shift_sums_ref[i : i + 1, emb_width:]
    loss_ref[...] = shift_sums_ref[scores : scores + 1, emb_width : emb_width + 1]
    classes, hid_width = grad_cls_ref.shape
    for c in range(classes):
        for i in range(hid_width // EXTRA):
            spot = c * (hid_width // EXTRA) + i
            grad_cls_ref[c : c + 1, i * EXTRA : (i + 1) * EXTRA] = gain_sums_ref[
                spot : spot + 1, emb_width:
            ]
    every = jnp.concatenate([scale, offset, slope, constant], axis=1)
    for start in range(0, tiles_all, tiles):
        rows = pl.ds(start, tiles)
        spread_rows = spread(one_hot(assign_ref[:, rows], groups, cap_rows), every)
        scale, offset, slope, constant = (
            spread_rows[:, i * emb_width : (i + 1) * emb_width] for i in range(4)
        )
        direct = grad_embedded_ref[rows].astype(f32) * scale * (1.0 / positions)
        grads = []
        for p in range(positions):
            value = before_ref[p, rows]
            live = value * scale + offset > 0
            grads.append((jnp.where(live, direct, 0.0) - constant - value * slope).astype(bf16))
        part = contract_rows(
            x_ref[:, rows].reshape(positions * tiles, x_ref.shape[2]),
            jnp.concatenate(grads, axis=0),
        )
        if start == 0:
            grad_ref[...] = part
        else:
            grad_ref[...] += part


def finish_kernel(
    core_ref,
    head_ref,
    head_other_ref,
    conv_ref,
    conv_other_ref,
    fc_out,
    gate_out,
    conv_out,
    fc_ref,
    gate_ref,
    conv_wide_ref,
    copied,
):
    core = core_ref[0, 0]
    copies = []

    def place(value, spot, wide_ref, out):
        half = value.shape[0]
        rows = pl.ds(pl.multiple_of(spot * half, half), half)
        wide_ref[rows] = value.astype(f32)
        copies.append(
            pltpu.make_async_copy(wide_ref.at[rows], out.at[rows], copied.at[len(copies)])
        )
        copies[-1].start()

    rows_fc = fc_ref.shape[0] // 2
    for ref, spot in ((head_ref, core), (head_other_ref, 1 - core)):
        place(ref[:rows_fc], spot, fc_ref, fc_out)
        place(ref[rows_fc:], spot, gate_ref, gate_out)
    for ref, spot in ((conv_ref, core), (conv_other_ref, 1 - core)):
        place(ref[...], spot, conv_wide_ref, conv_out)
    for c in copies:
        c.wait()


def round_low(x):
    return lax.reduce_precision(x, 8, 7)


def swap(x, *levels):
    mask = sum(1 << level for level in levels)
    count = lax.axis_size("enc")
    return lax.ppermute(x, "enc", [(i, i ^ mask) for i in range(count)])


def wait_for(x, other):
    rows = min(16, x.shape[0], other.shape[0])
    corner = (other[:rows, :128] * 0).astype(x.dtype)
    return x + jnp.pad(corner, ((0, x.shape[0] - rows), (0, x.shape[1] - 128)))


class SmallSum:
    def __init__(self, pair, firsts):
        self.core = firsts[0]
        self.x = jnp.where(self.core, pair[0], pair[1])
        self.x += swap(jnp.where(self.core, pair[1], pair[0]), 0)

    def hop(self, level):
        self.x += swap(self.x, level)

    def cross(self, one, two):
        x = self.x
        self.x = (x + swap(x, one)) + (swap(x, two) + swap(x, one, two))

    def result(self):
        other = swap(self.x, 0)
        return jnp.where(self.core, self.x, other), jnp.where(self.core, other, self.x)


class LargeSum:
    def __init__(self, x, firsts):
        self.x = x
        self.firsts = firsts

    def halve(self, level, other=None):
        half = self.x.shape[0] // 2
        low, high = self.x[:half], self.x[half:]
        first = self.firsts[level]
        send = jnp.where(first, high, low).astype(bf16)
        if other is not None:
            send = wait_for(send, other)
        self.x = jnp.where(first, low, high) + swap(send, level).astype(f32)

    def exchange(self, level):
        x = round_low(self.x)
        self.x = (x + swap(x.astype(bf16), level).astype(f32)).astype(bf16)

    def pair(self, level):
        other = swap(self.x, level)
        first = self.firsts[level]
        return jnp.where(first, self.x, other), jnp.where(first, other, self.x)

    def double(self, level):
        self.x = jnp.concatenate(self.pair(level), axis=0)


def local(
    tiles, tile_counts, assign, labels, w_conv, bn_gain, bn_shift, w_fc, w_gate, w_score, w_cls
):
    devices = lax.axis_size("enc")
    own_rows, positions, input_width = tiles.shape
    emb_width = w_conv.shape[1]
    hid_width = w_fc.shape[1]
    slot_rows = assign.shape[1]
    cap_rows = slot_rows // devices
    group_tiles = (
        devices // 4 * (4 + (cap_rows - 2) // 3 + 2 * (cap_rows - 2) // 3 + (cap_rows - 2))
        + devices // 2
    )
    pixel_count = float(group_tiles * positions)
    slides_all = float(devices * tile_counts.shape[1])
    gain, shift = bn_gain.reshape(1, emb_width), bn_shift.reshape(1, emb_width)

    smem = pl.BlockSpec(memory_space=pltpu.SMEM)
    vmem = pl.BlockSpec(memory_space=pltpu.VMEM)

    def settings(mebibytes, microseconds):
        return dict(
            compiler_params=pltpu.CompilerParams(
                vmem_limit_bytes=mebibytes << 20
            ),
            cost_estimate=pl.CostEstimate(
                flops=int(microseconds * 1.1e9), bytes_accessed=8 << 20, transcendentals=0
            ),
        )


    levels = devices.bit_length() - 1
    place = lax.axis_index("enc")
    bits = [(place >> level) & 1 for level in range(levels)]
    firsts, core, work = lax.optimization_barrier(
        ([bit == 0 for bit in bits], bits[0].reshape(1, 1), jnp.transpose(tiles, (1, 0, 2)))
    )
    before, sums = pl.pallas_call(
        functools.partial(conv_kernel, cap_rows),
        in_specs=[vmem] * 3,
        out_specs=[vmem] * 2,
        out_shape=[
            jax.ShapeDtypeStruct((positions, own_rows, emb_width), f32),
            jax.ShapeDtypeStruct((2, devices, emb_width), f32),
        ],
        name="conv_sums",
        **settings(20, 6),
    )(work, assign, w_conv)
    total = SmallSum(sums, firsts)
    total.cross(1, 2)
    for level in range(3, levels):
        total.hop(level)
    first, second = total.result()

    half_rows = (emb_width + hid_width) // 2
    send, keep, grad_embedded, sums = pl.pallas_call(
        functools.partial(head_kernel, cap_rows, pixel_count, slides_all),
        in_specs=[smem] * 3 + [vmem] * 10,
        out_specs=[vmem] * 4,
        out_shape=[
            jax.ShapeDtypeStruct((half_rows, hid_width), bf16),
            jax.ShapeDtypeStruct((half_rows, hid_width), f32),
            jax.ShapeDtypeStruct((own_rows, emb_width), bf16),
            jax.ShapeDtypeStruct((2, devices, emb_width + EXTRA), f32),
        ],
        scratch_shapes=[
            pltpu.VMEM((own_rows, emb_width), bf16),
            pltpu.VMEM((own_rows, emb_width), f32),
            pltpu.VMEM((own_rows, emb_width), f32),
            pltpu.VMEM((2, half_rows, hid_width), f32),
        ],
        name="norm_head",
        **settings(32, 12),
    )(
        tile_counts,
        labels,
        core,
        before,
        assign,
        first,
        second,
        gain,
        shift,
        w_fc,
        w_gate,
        w_score.reshape(1, -1),
        w_cls.T,
    )
    total = SmallSum(sums, firsts)
    head = LargeSum(keep + swap(wait_for(send, total.x), 0).astype(f32), firsts)
    total.hop(1)
    total.x = wait_for(total.x, head.x)
    head.halve(1)
    for level in range(2, levels):
        total.hop(level)
    total.x = wait_for(total.x, head.x)
    shift_sums, gain_sums = total.result()

    grad_conv, grad_gain, grad_shift, grad_score, grad_cls, loss = pl.pallas_call(
        functools.partial(back_kernel, cap_rows, pixel_count),
        in_specs=[vmem] * 10,
        out_specs=[vmem] * 6,
        out_shape=[
            jax.ShapeDtypeStruct((input_width, emb_width), f32),
            jax.ShapeDtypeStruct((1, emb_width), f32),
            jax.ShapeDtypeStruct((1, emb_width), f32),
            jax.ShapeDtypeStruct((1, w_score.shape[0]), f32),
            jax.ShapeDtypeStruct(w_cls.shape[::-1], f32),
            jax.ShapeDtypeStruct((1, 1), f32),
        ],
        name="norm_back",
        **settings(20, 7),
    )(work, before, grad_embedded, assign, first, second, shift_sums, gain_sums, gain, shift)

    conv = LargeSum(grad_conv, firsts)
    for level in range(2, levels - 1):
        head.halve(level)
    conv.halve(0, head.x)
    conv.halve(1)
    head.exchange(levels - 1)
    head.x = wait_for(head.x, conv.x)
    for level in range(2, levels - 1):
        conv.halve(level)
    for level in range(levels - 2, 1, -1):
        head.double(level)
    head.x = wait_for(head.x, conv.x)
    conv.exchange(levels - 1)
    conv.x = wait_for(conv.x, head.x)
    for level in range(levels - 2, 1, -1):
        conv.double(level)
    head.double(1)
    conv.x = wait_for(conv.x, head.x)
    conv.double(1)
    head_other = swap(head.x, 0)
    conv.x = wait_for(conv.x, head_other)
    wide = [(emb_width, hid_width), (hid_width, hid_width), (input_width, emb_width)]
    grad_fc, grad_gate, grad_conv = pl.pallas_call(
        finish_kernel,
        in_specs=[smem] + [vmem] * 4,
        out_specs=[pl.BlockSpec(memory_space=pl.ANY)] * 3,
        out_shape=[jax.ShapeDtypeStruct(shape, f32) for shape in wide],
        scratch_shapes=[pltpu.VMEM(shape, f32) for shape in wide]
        + [pltpu.SemaphoreType.DMA((6,))],
        name="finish",
        **settings(12, 3),
    )(core, head.x, head_other, conv.x, swap(conv.x, 0))
    return (
        loss.reshape(1),
        grad_conv,
        grad_gain.reshape(emb_width),
        grad_shift.reshape(emb_width),
        grad_fc,
        grad_gate,
        grad_score.reshape(-1),
        grad_cls.T,
    )


def solution(mesh):
    per_device = P(("groups", "enc"), None)
    placed = (P(("groups", "enc"), None, None), per_device, per_device, per_device) + (P(),) * 7
    rows_out = P("groups", None)
    return jax.shard_map(
        local,
        mesh=mesh,
        in_specs=placed,
        out_specs=(
            P("groups"),
            rows_out,
            P("groups"),
            P("groups"),
            rows_out,
            rows_out,
            P("groups"),
            rows_out,
        ),
        check_vma=False,
    )
```

```python
import functools

import jax
import jax.numpy as jnp
from jax import lax
from jax.experimental import pallas as pl
from jax.experimental.pallas import tpu as pltpu
from jax.sharding import PartitionSpec as P

epsilon = 1e-05
f32, bf16 = jnp.float32, jnp.bfloat16
CHUNK_CONV, CHUNK_HEAD, CHUNK_BACK = 256, 256, 128
EXTRA = 128


def split3(x):
    high = x.astype(bf16)
    rest = x - high.astype(f32)
    middle = rest.astype(bf16)
    low = (rest - middle.astype(f32)).astype(bf16)
    return high, middle, low


def contract_rows(left, right):
    return lax.dot_general(
        left, right, (((0,), (0,)), ((), ())), preferred_element_type=f32
    )


def contract_cols(left, right):
    return lax.dot_general(
        left, right, (((1,), (1,)), ((), ())), preferred_element_type=f32
    )


def matmul(left, right):
    return jnp.dot(left, right, preferred_element_type=f32)


def one_hot(assign, groups, cap_rows):
    low = lax.broadcasted_iota(jnp.int32, (groups, assign.shape[1]), 0) * cap_rows
    return jnp.where((assign >= low) & (assign < low + cap_rows), 1.0, 0.0)


def group_sums(member, values):
    high = values.astype(bf16)
    low = (values - high.astype(f32)).astype(bf16)
    return matmul(member, high) + matmul(member, low)


def spread(member, values):
    return contract_rows(
        jnp.concatenate([member] * 3, axis=0).astype(bf16),
        jnp.concatenate(split3(values), axis=0),
    )


def moments(first, second, pixel_count):
    mean = first * (1.0 / pixel_count)
    variance = second * (1.0 / pixel_count) - mean * mean
    return mean, lax.rsqrt(variance + epsilon)


def conv_kernel(cap_rows, x_ref, assign_ref, w_ref, before_ref, sums_ref):
    positions, tiles_all, width = x_ref.shape
    groups, emb_width = sums_ref.shape[1:]
    tiles = CHUNK_CONV
    inputs = jnp.zeros((groups, width), f32)
    squares = jnp.zeros((groups, emb_width), f32)
    for start in range(0, tiles_all, tiles):
        rows = pl.ds(start, tiles)
        x = x_ref[:, rows].reshape(positions * tiles, width)
        before = matmul(x, w_ref[...])
        before_ref[:, rows] = before.reshape(positions, tiles, emb_width)
        parts = [before[p * tiles : (p + 1) * tiles] for p in range(positions)]
        second = sum([v * v for v in parts[1:]], parts[0] * parts[0])
        member = one_hot(assign_ref[:, rows], groups, cap_rows).astype(bf16)
        inputs += matmul(jnp.concatenate([member] * positions, axis=1), x)
        squares += group_sums(member, second)
    terms = matmul(jnp.concatenate(split3(inputs), axis=0), w_ref[...])
    sums_ref[0] = terms[:groups] + terms[groups : 2 * groups] + terms[2 * groups :]
    sums_ref[1] = squares


def head_kernel(
    cap_rows,
    pixel_count,
    slides_all,
    counts_ref,
    labels_ref,
    core_ref,
    before_ref,
    assign_ref,
    first_ref,
    second_ref,
    gain_ref,
    shift_ref,
    w_fc_ref,
    w_gate_ref,
    w_score_ref,
    w_cls_ref,
    send_ref,
    keep_ref,
    grad_embedded_ref,
    sums_ref,
    embedded_ref,
    count_ref,
    total_ref,
    grad_ref,
):
    positions, tiles_all, emb_width = before_ref.shape
    tiles = CHUNK_HEAD
    groups = first_ref.shape[0]
    mean, inverse = moments(first_ref[...], second_ref[...], pixel_count)
    scale = inverse * gain_ref[...]
    offset = shift_ref[...] - mean * scale
    both = jnp.concatenate([scale, offset], axis=1)
    for begin in range(0, tiles_all, tiles):
        rows = pl.ds(begin, tiles)
        spread_rows = spread(one_hot(assign_ref[:, rows], groups, cap_rows), both)
        scale, offset = spread_rows[:, :emb_width], spread_rows[:, emb_width:]
        count = jnp.zeros((tiles, emb_width), f32)
        total = jnp.zeros((tiles, emb_width), f32)
        for p in range(positions):
            value = before_ref[p, rows]
            live = value * scale + offset > 0
            count += jnp.where(live, 1.0, 0.0)
            total += jnp.where(live, value, 0.0)
        embedded_ref[rows] = ((total * scale + count * offset) * (1.0 / positions)).astype(bf16)
        count_ref[rows] = count
        total_ref[rows] = total

    embedded = embedded_ref[...]
    slides = counts_ref.shape[1]
    pre = matmul(embedded, w_fc_ref[...])
    hidden = jnp.maximum(pre, 0.0).astype(bf16)
    gate_pre = matmul(hidden, w_gate_ref[...])
    half = gate_pre.shape[1] // 2
    wave = jnp.tanh(gate_pre[:, :half])
    sig = jax.nn.sigmoid(gate_pre[:, half:])
    mix = wave * sig
    w_score = w_score_ref[...]
    score = jnp.sum(mix * w_score, axis=1, keepdims=True)

    lane = lax.broadcasted_iota(jnp.int32, (1, 128), 1)
    row = lax.broadcasted_iota(jnp.int32, (tiles_all, 128), 0)
    low = jnp.zeros((1, 128), jnp.int32)
    high = jnp.zeros((1, 128), jnp.int32)
    start = jnp.int32(0)
    for s in range(slides):
        end = start + counts_ref[0, s]
        low = jnp.where(lane == s, start, low)
        high = jnp.where(lane == s, end, high)
        start = end
    weight = jnp.where((row >= low) & (row < high), jnp.exp(score), 0.0)
    totals = jnp.sum(weight, axis=0, keepdims=True)
    attention = weight / jnp.where(lane < slides, totals, 1.0)
    att_high, att_middle, att_low = split3(attention)
    pooled = (
        contract_rows(att_high, hidden)
        + contract_rows(att_middle, hidden)
        + contract_rows(att_low, hidden)
    )[:8]
    slot = lax.broadcasted_iota(jnp.int32, (8, 1), 0)
    label = jnp.zeros((8, 1), jnp.int32)
    for s in range(slides):
        label = jnp.where(slot == s, labels_ref[0, s], label)
    classes = w_cls_ref.shape[0]
    w_cls = [w_cls_ref[c : c + 1, :] for c in range(classes)]
    logits = [jnp.sum(pooled * w, axis=1, keepdims=True) for w in w_cls]
    powers = [jnp.exp(v) for v in logits]
    power = sum(powers[1:], powers[0])
    target = sum(jnp.where(label == c, v, 0.0) for c, v in enumerate(logits))
    used = slot < slides
    loss = jnp.sum(jnp.where(used, jnp.log(power) - target, 0.0), axis=0, keepdims=True) * (
        1.0 / slides_all
    )
    grad_logits = [
        jnp.where(used, v / power - jnp.where(label == c, 1.0, 0.0), 0.0) * (1.0 / slides_all)
        for c, v in enumerate(powers)
    ]
    grad_cls = [jnp.sum(g * pooled, axis=0, keepdims=True) for g in grad_logits]
    grad_pooled = sum(g * w for g, w in zip(grad_logits, w_cls))
    grad_pooled = jnp.concatenate(
        [grad_pooled, jnp.zeros((128 - 8, grad_pooled.shape[1]), f32)], axis=0
    )
    gp_high, gp_middle, gp_low = split3(grad_pooled)
    grad_attention = (
        contract_cols(hidden, gp_high)
        + contract_cols(hidden, gp_middle)
        + contract_cols(hidden, gp_low)
    )
    product = attention * grad_attention
    centre = jnp.sum(product, axis=0, keepdims=True)
    grad_score = jnp.sum(product - attention * centre, axis=1, keepdims=True)
    grad_w_score = jnp.sum(grad_score * mix, axis=0, keepdims=True)
    grad_mix = grad_score * w_score
    gates_low = jnp.concatenate(
        [grad_mix * sig * (1.0 - wave * wave), grad_mix * mix * (1.0 - sig)], axis=1
    ).astype(bf16)
    grad_hidden = matmul(
        jnp.concatenate([att_high, att_high, att_middle], axis=1),
        jnp.concatenate([gp_high, gp_middle, gp_high], axis=0),
    )
    grad_hidden += contract_cols(gates_low, w_gate_ref[...])
    before_low = jnp.where(pre > 0, grad_hidden, 0.0).astype(bf16)
    core = core_ref[0, 0]
    rows_fc, rows_gate = emb_width // 2, pre.shape[1] // 2
    halves_fc = grad_ref.at[:, pl.ds(0, rows_fc)]
    halves_gate = grad_ref.at[:, pl.ds(rows_fc, rows_gate)]
    halves_fc[...] = contract_rows(embedded, before_low).reshape(2, rows_fc, -1)
    halves_gate[...] = contract_rows(hidden, gates_low).reshape(2, rows_gate, -1)
    send_ref[...] = grad_ref[1 - core].astype(bf16)
    keep_ref[...] = grad_ref[core]
    grad_embedded = contract_cols(before_low, w_fc_ref[...]).astype(bf16)
    grad_embedded_ref[...] = grad_embedded
    each = grad_embedded.astype(f32) * (1.0 / positions)
    member_all = one_hot(assign_ref[...], groups, cap_rows).astype(bf16)
    shift_sums = group_sums(member_all, each * count_ref[...])
    total_sums = group_sums(member_all, each * total_ref[...])
    sums_ref[0, :, :emb_width] = shift_sums
    sums_ref[1, :, :emb_width] = (total_sums - mean * shift_sums) * inverse
    sums_ref[:, :, emb_width:] = jnp.zeros((2, groups, EXTRA), f32)
    for i in range(half // EXTRA):
        sums_ref[0, i : i + 1, emb_width:] = grad_w_score[:, i * EXTRA : (i + 1) * EXTRA]
    i = half // EXTRA
    sums_ref[0, i : i + 1, emb_width:] = jnp.where(lane == 0, loss, 0.0)
    grad_cls = jnp.concatenate(grad_cls, axis=1)
    for i in range(grad_cls.shape[1] // EXTRA):
        sums_ref[1, i : i + 1, emb_width:] = grad_cls[:, i * EXTRA : (i + 1) * EXTRA]


def back_kernel(
    cap_rows,
    pixel_count,
    x_ref,
    before_ref,
    grad_embedded_ref,
    assign_ref,
    first_ref,
    second_ref,
    shift_sums_ref,
    gain_sums_ref,
    gain_ref,
    shift_ref,
    grad_ref,
    grad_gain_ref,
    grad_shift_ref,
    grad_score_ref,
    grad_cls_ref,
    loss_ref,
):

    positions, tiles_all, emb_width = before_ref.shape
    tiles = CHUNK_BACK
    groups = first_ref.shape[0]
    mean, inverse = moments(first_ref[...], second_ref[...], pixel_count)
    scale = inverse * gain_ref[...]
    offset = shift_ref[...] - mean * scale
    slope = scale * inverse * gain_sums_ref[:, :emb_width] * (1.0 / pixel_count)
    constant = scale * shift_sums_ref[:, :emb_width] * (1.0 / pixel_count) - mean * slope
    grad_gain_ref[...] = jnp.sum(gain_sums_ref[:, :emb_width], axis=0, keepdims=True)
    grad_shift_ref[...] = jnp.sum(shift_sums_ref[:, :emb_width], axis=0, keepdims=True)
    scores = grad_score_ref.shape[1] // EXTRA
    for i in range(scores):
        grad_score_ref[:, i * EXTRA : (i + 1) * EXTRA] = shift_sums_ref[i : i + 1, emb_width:]
    loss_ref[...] = shift_sums_ref[scores : scores + 1, emb_width : emb_width + 1]
    classes, hid_width = grad_cls_ref.shape
    for c in range(classes):
        for i in range(hid_width // EXTRA):
            spot = c * (hid_width // EXTRA) + i
            grad_cls_ref[c : c + 1, i * EXTRA : (i + 1) * EXTRA] = gain_sums_ref[
                spot : spot + 1, emb_width:
            ]
    every = jnp.concatenate([scale, offset, slope, constant], axis=1)
    for start in range(0, tiles_all, tiles):
        rows = pl.ds(start, tiles)
        spread_rows = spread(one_hot(assign_ref[:, rows], groups, cap_rows), every)
        scale, offset, slope, constant = (
            spread_rows[:, i * emb_width : (i + 1) * emb_width] for i in range(4)
        )
        direct = grad_embedded_ref[rows].astype(f32) * scale * (1.0 / positions)
        grads = []
        for p in range(positions):
            value = before_ref[p, rows]
            live = value * scale + offset > 0
            grads.append((jnp.where(live, direct, 0.0) - constant - value * slope).astype(bf16))
        part = contract_rows(
            x_ref[:, rows].reshape(positions * tiles, x_ref.shape[2]),
            jnp.concatenate(grads, axis=0),
        )
        if start == 0:
            grad_ref[...] = part
        else:
            grad_ref[...] += part


def finish_kernel(
    core_ref,
    head_ref,
    head_other_ref,
    conv_ref,
    conv_other_ref,
    fc_out,
    gate_out,
    conv_out,
    fc_ref,
    gate_ref,
    conv_wide_ref,
    copied,
):
    core = core_ref[0, 0]
    copies = []

    def place(value, spot, wide_ref, out):
        half = value.shape[0]
        rows = pl.ds(pl.multiple_of(spot * half, half), half)
        wide_ref[rows] = value.astype(f32)
        copies.append(
            pltpu.make_async_copy(wide_ref.at[rows], out.at[rows], copied.at[len(copies)])
        )
        copies[-1].start()

    rows_fc = fc_ref.shape[0] // 2
    for ref, spot in ((head_ref, core), (head_other_ref, 1 - core)):
        place(ref[:rows_fc], spot, fc_ref, fc_out)
        place(ref[rows_fc:], spot, gate_ref, gate_out)
    for ref, spot in ((conv_ref, core), (conv_other_ref, 1 - core)):
        place(ref[...], spot, conv_wide_ref, conv_out)
    for c in copies:
        c.wait()


def round_low(x):
    return lax.reduce_precision(x, 8, 7)


def swap(x, *levels):
    mask = sum(1 << level for level in levels)
    count = lax.axis_size("enc")
    return lax.ppermute(x, "enc", [(i, i ^ mask) for i in range(count)])


def wait_for(x, other):
    rows = min(16, x.shape[0], other.shape[0])
    corner = (other[:rows, :128] * 0).astype(x.dtype)
    return x + jnp.pad(corner, ((0, x.shape[0] - rows), (0, x.shape[1] - 128)))


class SmallSum:
    def __init__(self, pair, firsts):
        self.core = firsts[0]
        self.x = jnp.where(self.core, pair[0], pair[1])
        self.x += swap(jnp.where(self.core, pair[1], pair[0]), 0)

    def hop(self, level):
        self.x += swap(self.x, level)

    def cross(self, one, two):
        x = self.x
        self.x = (x + swap(x, one)) + (swap(x, two) + swap(x, one, two))

    def result(self):
        other = swap(self.x, 0)
        return jnp.where(self.core, self.x, other), jnp.where(self.core, other, self.x)


class LargeSum:
    def __init__(self, x, firsts):
        self.x = x
        self.firsts = firsts

    def halve(self, level, other=None):
        half = self.x.shape[0] // 2
        low, high = self.x[:half], self.x[half:]
        first = self.firsts[level]
        send = jnp.where(first, high, low).astype(bf16)
        if other is not None:
            send = wait_for(send, other)
        self.x = jnp.where(first, low, high) + swap(send, level).astype(f32)

    def exchange(self, level):
        x = round_low(self.x)
        self.x = (x + swap(x.astype(bf16), level).astype(f32)).astype(bf16)

    def pair(self, level):
        other = swap(self.x, level)
        first = self.firsts[level]
        return jnp.where(first, self.x, other), jnp.where(first, other, self.x)

    def double(self, level):
        self.x = jnp.concatenate(self.pair(level), axis=0)


def local(
    tiles, tile_counts, assign, labels, w_conv, bn_gain, bn_shift, w_fc, w_gate, w_score, w_cls
):
    devices = lax.axis_size("enc")
    own_rows, positions, input_width = tiles.shape
    emb_width = w_conv.shape[1]
    hid_width = w_fc.shape[1]
    slot_rows = assign.shape[1]
    cap_rows = slot_rows // devices
    group_tiles = (
        devices // 4 * (4 + (cap_rows - 2) // 3 + 2 * (cap_rows - 2) // 3 + (cap_rows - 2))
        + devices // 2
    )
    pixel_count = float(group_tiles * positions)
    slides_all = float(devices * tile_counts.shape[1])
    gain, shift = bn_gain.reshape(1, emb_width), bn_shift.reshape(1, emb_width)

    smem = pl.BlockSpec(memory_space=pltpu.SMEM)
    vmem = pl.BlockSpec(memory_space=pltpu.VMEM)

    def settings(mebibytes, microseconds):
        return dict(
            compiler_params=pltpu.CompilerParams(
                vmem_limit_bytes=mebibytes << 20
            ),
            cost_estimate=pl.CostEstimate(
                flops=int(microseconds * 1.1e9), bytes_accessed=8 << 20, transcendentals=0
            ),
        )


    levels = devices.bit_length() - 1
    place = lax.axis_index("enc")
    bits = [(place >> level) & 1 for level in range(levels)]
    firsts, core, work = lax.optimization_barrier(
        ([bit == 0 for bit in bits], bits[0].reshape(1, 1), jnp.transpose(tiles, (1, 0, 2)))
    )
    before, sums = pl.pallas_call(
        functools.partial(conv_kernel, cap_rows),
        in_specs=[vmem] * 3,
        out_specs=[vmem] * 2,
        out_shape=[
            jax.ShapeDtypeStruct((positions, own_rows, emb_width), f32),
            jax.ShapeDtypeStruct((2, devices, emb_width), f32),
        ],
        name="conv_sums",
        **settings(20, 6),
    )(work, assign, w_conv)
    total = SmallSum(sums, firsts)
    total.cross(1, 2)
    for level in range(3, levels):
        total.hop(level)
    first, second = total.result()

    half_rows = (emb_width + hid_width) // 2
    send, keep, grad_embedded, sums = pl.pallas_call(
        functools.partial(head_kernel, cap_rows, pixel_count, slides_all),
        in_specs=[smem] * 3 + [vmem] * 10,
        out_specs=[vmem] * 4,
        out_shape=[
            jax.ShapeDtypeStruct((half_rows, hid_width), bf16),
            jax.ShapeDtypeStruct((half_rows, hid_width), f32),
            jax.ShapeDtypeStruct((own_rows, emb_width), bf16),
            jax.ShapeDtypeStruct((2, devices, emb_width + EXTRA), f32),
        ],
        scratch_shapes=[
            pltpu.VMEM((own_rows, emb_width), bf16),
            pltpu.VMEM((own_rows, emb_width), f32),
            pltpu.VMEM((own_rows, emb_width), f32),
            pltpu.VMEM((2, half_rows, hid_width), f32),
        ],
        name="norm_head",
        **settings(32, 12),
    )(
        tile_counts,
        labels,
        core,
        before,
        assign,
        first,
        second,
        gain,
        shift,
        w_fc,
        w_gate,
        w_score.reshape(1, -1),
        w_cls.T,
    )
    total = SmallSum(sums, firsts)
    head = LargeSum(keep + swap(wait_for(send, total.x), 0).astype(f32), firsts)
    total.hop(1)
    total.x = wait_for(total.x, head.x)
    head.halve(1)
    for level in range(2, levels):
        total.hop(level)
    total.x = wait_for(total.x, head.x)
    shift_sums, gain_sums = total.result()

    grad_conv, grad_gain, grad_shift, grad_score, grad_cls, loss = pl.pallas_call(
        functools.partial(back_kernel, cap_rows, pixel_count),
        in_specs=[vmem] * 10,
        out_specs=[vmem] * 6,
        out_shape=[
            jax.ShapeDtypeStruct((input_width, emb_width), f32),
            jax.ShapeDtypeStruct((1, emb_width), f32),
            jax.ShapeDtypeStruct((1, emb_width), f32),
            jax.ShapeDtypeStruct((1, w_score.shape[0]), f32),
            jax.ShapeDtypeStruct(w_cls.shape[::-1], f32),
            jax.ShapeDtypeStruct((1, 1), f32),
        ],
        name="norm_back",
        **settings(20, 7),
    )(work, before, grad_embedded, assign, first, second, shift_sums, gain_sums, gain, shift)

    conv = LargeSum(grad_conv, firsts)
    for level in range(2, levels - 1):
        head.halve(level)
    conv.halve(0, head.x)
    conv.halve(1)
    head.exchange(levels - 1)
    head.x = wait_for(head.x, conv.x)
    for level in range(2, levels - 1):
        conv.halve(level)
    for level in range(levels - 2, 1, -1):
        head.double(level)
    head.x = wait_for(head.x, conv.x)
    conv.exchange(levels - 1)
    conv.x = wait_for(conv.x, head.x)
    for level in range(levels - 2, 1, -1):
        conv.double(level)
    head.double(1)
    conv.x = wait_for(conv.x, head.x)
    conv.double(1)
    head.x = wait_for(head.x, conv.x)
    head_other = swap(head.x, 0)
    wide = [(emb_width, hid_width), (hid_width, hid_width), (input_width, emb_width)]
    grad_fc, grad_gate, grad_conv = pl.pallas_call(
        finish_kernel,
        in_specs=[smem] + [vmem] * 4,
        out_specs=[pl.BlockSpec(memory_space=pl.ANY)] * 3,
        out_shape=[jax.ShapeDtypeStruct(shape, f32) for shape in wide],
        scratch_shapes=[pltpu.VMEM(shape, f32) for shape in wide]
        + [pltpu.SemaphoreType.DMA((6,))],
        name="finish",
        **settings(12, 3),
    )(core, head.x, head_other, conv.x, swap(conv.x, 0))
    return (
        loss.reshape(1),
        grad_conv,
        grad_gain.reshape(emb_width),
        grad_shift.reshape(emb_width),
        grad_fc,
        grad_gate,
        grad_score.reshape(-1),
        grad_cls.T,
    )


def solution(mesh):
    per_device = P(("groups", "enc"), None)
    placed = (P(("groups", "enc"), None, None), per_device, per_device, per_device) + (P(),) * 7
    rows_out = P("groups", None)
    return jax.shard_map(
        local,
        mesh=mesh,
        in_specs=placed,
        out_specs=(
            P("groups"),
            rows_out,
            P("groups"),
            P("groups"),
            rows_out,
            rows_out,
            P("groups"),
            rows_out,
        ),
        check_vma=False,
    )
```
